512 devices in a mesh: chan: 32 (over x, z_lo), tm: 16 (over y, z_hi, core).
Axes of the slice: x: 4, y: 4, z: 16 (z_hi: 2, z_lo: 8; z = z_hi * 8 + z_lo), core: 2. Of those that a mesh axis runs over, the one named last changes fastest.
Arguments:
- records: bfloat16 [512, 16, 768], P('chan', 'tm'), may hold values from -64 to 64
- source_ids: int32 [2, 128], replicated, may hold values from 0 to 511, as said below
- pair_rows: int32 [2, 16384], P(None, 'chan'), may hold values from 0 to 2047, as said below
- pair_bins: int32 [2, 16384], P(None, 'chan'), may hold values from 0 to 511, as said below
- bin_places: int32 [512], replicated, may hold values from 0 to 511, as said below
Outputs:
- stacks: float32 [512, 1024], P('tm', 'chan')
The draws below stay inside these ranges and needn't reach their ends.
Inputs may be any that keep to these rules, and one draw needn't show every extreme that they name: `source_ids`: in each step the 128 ids are distinct. `pair_rows`: within each step, the 512 entries of one block of columns are distinct. `pair_bins`: within each step and block of 512 columns, at most 64 entries name bins whose owner bin_places // 32 is the same, and one owner is named by exactly 64. `bin_places`: each bin has its own row: the entries are a permutation.
All inputs are finite; a program needn't handle non-finite values.
Results may differ from the reference program's by a relative error of at most 0.004.
Values may be sent and summed in bfloat16 or wider, within the bound.
No kernel may reach another device: no remote copies, remote signals or barrier semaphores. Data moves between devices by JAX's collectives and lax.ppermute only.
A program may use at most 64 MiB of HBM per device.

```python
import math
import jax
import jax.numpy as jnp
from jax import lax

NT = 768
LAGS = 1024
SRC = 128
STEPS = 2
CH_DEV = 16
BIN_DEV = 32
PAIR_DEV = 512
CHANNELS = 512
WINDOWS = 16
BINS = 512


def draw_records(key, part):
    scale_key, value_key = jax.random.split(jax.random.fold_in(key, 11))
    full_shape = (CHANNELS, WINDOWS, NT)
    levels = jnp.exp(jax.random.uniform(scale_key, (CHANNELS, WINDOWS, 1), jnp.float32, 0.0, math.log(10.0)))
    values = jnp.clip(jax.random.normal(value_key, full_shape, jnp.float32), -4.0, 4.0)
    return (levels * values).astype(jnp.bfloat16)


def draw_source_ids(key, part):

    def one_step(step_key):
        return jax.random.permutation(step_key, CHANNELS)[:SRC].astype(jnp.int32)
    return jax.vmap(one_step)(jax.random.split(jax.random.fold_in(key, 21), STEPS))


def draw_pair_rows(key, part):
    block_total = CHANNELS // CH_DEV

    def one_block(block_key):
        return jax.random.permutation(block_key, CH_DEV * SRC)[:PAIR_DEV].astype(jnp.int32)
    picks = jax.vmap(one_block)(jax.random.split(jax.random.fold_in(key, 31), STEPS * block_total))
    return picks.reshape(STEPS, block_total * PAIR_DEV)


def bin_order(key):
    return jax.random.permutation(jax.random.fold_in(key, 41), BINS).astype(jnp.int32)


def draw_bin_places(key, part):
    return bin_order(key)


def draw_pair_bins(key, part):
    block_total = CHANNELS // CH_DEV
    owner_total = BINS // BIN_DEV
    capacity = 2 * PAIR_DEV // owner_total
    inverse = jnp.argsort(bin_order(key), stable=True).astype(jnp.int32)
    position = jnp.arange(PAIR_DEV)

    def one_block(block_key):
        busy_key, order_key, slot_key = jax.random.split(block_key, 3)
        busiest = jax.random.randint(busy_key, (), 0, owner_total)
        spread = (busiest + 1 + (position - capacity) % max(owner_total - 1, 1)) % owner_total
        owners = jnp.where(position < capacity, busiest, spread)
        owners = owners[jax.random.permutation(order_key, PAIR_DEV)]
        slots = jax.random.randint(slot_key, (PAIR_DEV,), 0, BIN_DEV)
        return inverse[owners * BIN_DEV + slots].astype(jnp.int32)
    picks = jax.vmap(one_block)(jax.random.split(jax.random.fold_in(key, 51), STEPS * block_total))
    return picks.reshape(STEPS, block_total * PAIR_DEV)


def setup_inputs(seed: int = 0) -> dict:
    splits = jax.random.split(jax.random.key(seed), 6)
    records = draw_records(jax.random.fold_in(splits[5], 71), 0)
    source_ids = draw_source_ids(jax.random.fold_in(splits[5], 71), 0)
    pair_rows = draw_pair_rows(jax.random.fold_in(splits[5], 71), 0)
    pair_bins = draw_pair_bins(jax.random.fold_in(splits[5], 71), 0)
    bin_places = draw_bin_places(jax.random.fold_in(splits[5], 71), 0)
    return {"records": records, "source_ids": source_ids, "pair_rows": pair_rows, "pair_bins": pair_bins, "bin_places": bin_places}


def normalize(records):
    values = records.astype(jnp.float32)
    mean_square = lax.optimization_barrier(jnp.mean(values * values, axis=-1, keepdims=True))
    return (values * lax.rsqrt(mean_square + 1e-06)).astype(jnp.bfloat16)

def reference(records, source_ids, pair_rows, pair_bins, bin_places):
    normed = normalize(records)
    fourier_size = 1 << (NT + LAGS - 1).bit_length()
    half_lag = LAGS // 2
    column_count = pair_rows.shape[1]
    block_base = (jnp.arange(column_count) // PAIR_DEV * (CH_DEV * SRC)).astype(jnp.int32)
    totals = jnp.zeros((BINS, LAGS), jnp.float32)
    for step_index in range(STEPS):
        sources = jnp.take(normed, source_ids[step_index], axis=0)

        def window_corr(running, window):
            receivers = lax.dynamic_index_in_dim(normed, window, axis=1, keepdims=False).astype(jnp.float32)
            emitters = lax.dynamic_index_in_dim(sources, window, axis=1, keepdims=False).astype(jnp.float32)
            recv_spec = jnp.fft.rfft(receivers, n=fourier_size)
            emit_spec = jnp.fft.rfft(emitters, n=fourier_size)
            circular = jnp.fft.irfft(jnp.conj(recv_spec)[:, None, :] * emit_spec[None, :, :], n=fourier_size)
            lagged = jnp.roll(circular, half_lag, axis=-1)[..., :LAGS]
            return (running + lagged.astype(jnp.float32), None)
        summed, _ = lax.scan(window_corr, jnp.zeros((CHANNELS, SRC, LAGS), jnp.float32), jnp.arange(WINDOWS))
        lag_rows = summed.reshape(CHANNELS * SRC, LAGS)
        picked = jnp.take(lag_rows, pair_rows[step_index] + block_base, axis=0)
        totals = totals + jax.ops.segment_sum(picked, bin_places[pair_bins[step_index]], num_segments=BINS)
    return totals / NT
```

```python
import functools

import jax
import jax.numpy as jnp
import numpy as np
from jax import lax
from jax.experimental import pallas as pl
from jax.experimental.pallas import tpu as pltpu
from jax.sharding import Mesh, PartitionSpec as P

NT = 768
LAGS = 1024
SRC = 128
CH_DEV = 16
CHANNELS = 512
BIN_DEV = 32
BINS = 512
PAIRS = 1024
NFFT = 2048
PARTS = 8
SLOTS = NFFT // 4 // PARTS
LANES = 128
WIDE = 2 * LANES

bf16 = jnp.bfloat16
f32 = jnp.float32
dot = functools.partial(jnp.dot, preferred_element_type=f32)
HBM = pl.BlockSpec(memory_space=pltpu.MemorySpace.HBM)
VMEM = pl.BlockSpec(memory_space=pltpu.VMEM)
SMEM = pl.BlockSpec(memory_space=pltpu.SMEM)


def angles(left, right):
    return (np.outer(left, right) % (2 * NFFT)) * (np.pi / NFFT)


def forward_table():
    phase = angles(np.arange(NT), 2 * np.arange(NFFT // 4) + 1)
    return np.concatenate([np.cos(phase), np.sin(phase)], axis=1).astype(bf16)


def inverse_tables():
    lag = np.arange(LAGS) - LAGS // 2
    phase = angles(2 * np.arange(SLOTS) + 1, lag)
    turn = angles(np.arange(PARTS) * 2 * SLOTS, lag)
    scale = 2.0 / (NFFT * NT)
    sign = 1 - 2 * (lag % 2)
    cos, sin = np.cos(phase), np.sin(phase)
    base = np.concatenate([cos, sign * cos, sin, sign * sin], axis=0).astype(bf16)
    turns = scale * np.stack([np.cos(turn), np.sin(turn)], axis=1)
    return base, turns.astype(np.float32)


def spectra_kernel(records_hbm, table_hbm, rows_hbm, bins_hbm, places_hbm, out_ref, *scratch):
    *refs, sems = scratch
    sources = (rows_hbm, bins_hbm, places_hbm, records_hbm, table_hbm)
    copies = [pltpu.make_async_copy(s, d, sems.at[i]) for i, (s, d) in enumerate(zip(sources, refs))]
    for copy in copies:
        copy.start()
    rows_ref, bins_ref, places_ref, records_ref, table_ref = refs
    for copy in copies[:3]:
        copy.wait()

    place = places_ref[...]
    owner, slot = place // BIN_DEV, place % BIN_DEV
    order = (slot // 8) * 128 + (owner // 4) * 32 + (owner % 2) * 16
    order = order + (slot % 4) * 4 + ((owner // 2) % 2) * 2 + (slot // 4) % 2
    digits = jnp.broadcast_to(order - BINS // 2, (8, BINS)).astype(f32).astype(bf16)
    bins = jnp.concatenate([bins_ref[0:1, :], bins_ref[1:2, :]], axis=1)
    match = lax.broadcasted_iota(jnp.int32, (BINS, PAIRS), 0) == bins
    spots = dot(digits, match.astype(f32).astype(bf16))[0:1]
    rows = jnp.concatenate([rows_ref[0:1, :], rows_ref[1:2, :]], axis=1)
    lists = [(rows // SRC).astype(f32), (rows % SRC).astype(f32), spots, spots]
    packed = [item[:, 256 * j : 256 * (j + 1)] for item in lists for j in range(4)]
    packed = jnp.concatenate(packed, axis=0).astype(bf16)

    copies[3].wait()
    values = records_ref[...].astype(f32)
    mean_square = jnp.mean(values * values, axis=-1, keepdims=True)
    normed = values * lax.rsqrt(mean_square + 1e-06)
    odd = lax.broadcasted_iota(jnp.int32, normed.shape, 1) % 2 == 1
    split = jnp.concatenate([jnp.where(odd, 0.0, normed), jnp.where(odd, normed, 0.0)], axis=0).astype(bf16)
    copies[4].wait()
    sums = dot(split, table_ref[...])
    even, odd = sums[:CH_DEV], sums[CH_DEV:]
    lower, upper = even + odd, even - odd
    half = PARTS * SLOTS
    for z in range(PARTS):
        cuts = [slice(start + SLOTS * z, start + SLOTS * (z + 1)) for start in (0, half)]
        part = jnp.concatenate([piece[:, cut] for cut in cuts for piece in (lower, upper)], axis=1)
        out_ref[z, :CH_DEV, :] = part.astype(bf16)
        out_ref[z, CH_DEV:, :] = packed


def make_spectra(records, rows, bins, places):
    table = jnp.asarray(forward_table())
    inputs = (rows, bins, places, records, table)
    return pl.pallas_call(
        spectra_kernel,
        out_shape=jax.ShapeDtypeStruct((PARTS, 2 * CH_DEV, WIDE), bf16),
        in_specs=[HBM] * 5,
        out_specs=VMEM,
        scratch_shapes=[pltpu.VMEM(item.shape, item.dtype) for item in inputs] + [pltpu.SemaphoreType.DMA((5,))],
        name="spectra",
    )(records, table, rows, bins, places)


def pairs_kernel(own_ref, all_ref, ids_ref, out_ref, src_ref, recv_ref, total_ref):
    ids = jnp.concatenate([ids_ref[...].astype(f32)] + [jnp.zeros((6, SRC), f32)], axis=0).T
    lane = lax.broadcasted_iota(jnp.int32, (SRC, CHANNELS), 1).astype(f32)
    for k in range(2):
        pick = (ids[:, k : k + 1] == lane).astype(f32).astype(bf16)
        src_ref[k] = dot(pick, all_ref[...]).astype(bf16)
    for z in range(PARTS):
        recv_ref[CH_DEV * z : CH_DEV * (z + 1), :] = own_ref[z, :CH_DEV, :]
    lane = lax.broadcasted_iota(jnp.int32, (256, SRC), 1).astype(f32)
    bin_row = (lax.broadcasted_iota(jnp.int32, (BINS, 256), 0) - BINS // 2).astype(f32).astype(bf16)
    one, zero = jnp.ones((BINS, 256), bf16), jnp.zeros((BINS, 256), bf16)
    for z in range(PARTS):
        lists = own_ref[z, CH_DEV:, :]
        columns = lists.astype(f32).T
        products, matches = [], []
        for j in range(4):
            pick_r = (columns[:, j : j + 1] + float(z * CH_DEV) == lane).astype(f32).astype(bf16)
            pick_s = (columns[:, 4 + j : 5 + j] == lane).astype(f32).astype(bf16)
            r, s = dot(pick_r, recv_ref[...]), dot(pick_s, src_ref[j // 2])
            rc, rs, sc, ss = r[:, :LANES], r[:, LANES:], s[:, :LANES], s[:, LANES:]
            product = jnp.concatenate([rc * sc + rs * ss, rs * sc - rc * ss], axis=1)
            products.append(product.astype(bf16))
            matches.append(jnp.where(bin_row == lists[8 + j : 9 + j, :], one, zero))
        part = dot(jnp.concatenate(matches, axis=1), jnp.concatenate(products, axis=0))
        if z == 0:
            total_ref[...] = part
        elif z < PARTS - 1:
            total_ref[...] += part
        else:
            out_ref[...] = (total_ref[...] + part).astype(bf16)


def bin_pairs(own, everyone, ids):
    return pl.pallas_call(
        pairs_kernel,
        out_shape=jax.ShapeDtypeStruct((BINS, WIDE), bf16),
        in_specs=[VMEM, VMEM, VMEM],
        out_specs=VMEM,
        scratch_shapes=[
            pltpu.VMEM((2, SRC, WIDE), bf16),
            pltpu.VMEM((PARTS * CH_DEV, WIDE), bf16),
            pltpu.VMEM((BINS, WIDE), f32),
        ],
        compiler_params=pltpu.CompilerParams(vmem_limit_bytes=32 << 20),
        name="bin_pairs",
    )(own, everyone, ids)


def inverse_kernel(part_ref, parts_ref, base_ref, turns_ref, out_ref):
    spectrum = jnp.sum(parts_ref[...].astype(f32), axis=0)
    high = spectrum.astype(bf16)
    low = (spectrum - high.astype(f32)).astype(bf16)
    both = jnp.concatenate([high, low], axis=0)
    re, im = both[:, :LANES], both[:, LANES:]
    cos, sin = base_ref[:LANES, :], base_ref[LANES:, :]
    real = dot(re, cos) - dot(im, sin)
    imag = dot(re, sin) + dot(im, cos)
    turns = turns_ref[part_ref[0]]
    lags = (real[:16] + real[16:]) * turns[0:1] - (imag[:16] + imag[16:]) * turns[1:2]
    for group in range(8):
        tile = lags[:, 128 * group : 128 * (group + 1)]
        for quarter in range(4):
            lane = slice(32 * quarter, 32 * (quarter + 1))
            out_ref[4 * group + quarter] = jnp.concatenate([tile[4 * c : 4 * c + 4, lane] for c in range(4)], axis=1)


def invert(parts):
    base, turns = inverse_tables()
    part = lax.axis_index("zl").astype(jnp.int32).reshape(1)
    return pl.pallas_call(
        inverse_kernel,
        out_shape=jax.ShapeDtypeStruct((32, 4, 128), f32),
        in_specs=[SMEM, VMEM, VMEM, VMEM],
        out_specs=VMEM,
        compiler_params=pltpu.CompilerParams(vmem_limit_bytes=32 << 20),
        name="invert",
    )(part, parts, jnp.asarray(base), jnp.asarray(turns))


def exchange(value, axes):
    return lax.all_to_all(value, axes, split_axis=0, concat_axis=0, tiled=True)


def shards(records, source_ids, pair_rows, pair_bins, bin_places):
    spectra = make_spectra(records.reshape(CH_DEV, NT), pair_rows, pair_bins, bin_places.reshape(1, BINS))
    own = exchange(spectra, "zl")
    offered = own[:, :CH_DEV, :].reshape(1, SRC, WIDE)
    everyone = exchange(jnp.broadcast_to(offered, (4, SRC, WIDE)), "x").reshape(CHANNELS, WIDE)
    binned = bin_pairs(own, everyone, source_ids)
    parts = exchange(binned.reshape(32, 16, WIDE), ("x", "y", "core"))
    shares = exchange(invert(parts).reshape(64, 2, 128), ("x", "zl", "zh"))
    return jnp.sum(shares.reshape(4, 16, 2, 128), axis=1).reshape(BIN_DEV, 32)


def solution(mesh):
    fine = Mesh(mesh.devices.reshape(4, 8, 4, 2, 2), ("x", "zl", "y", "zh", "core"))
    chan, tm = ("x", "zl"), ("y", "zh", "core")
    in_specs = (P(chan, tm, None), P(), P(None, chan), P(None, chan), P())
    return jax.shard_map(shards, mesh=fine, in_specs=in_specs, out_specs=P(tm, chan), check_vma=False)
```

```python
import functools

import jax
import jax.numpy as jnp
import numpy as np
from jax import lax
from jax.experimental import pallas as pl
from jax.experimental.pallas import tpu as pltpu
from jax.sharding import Mesh, PartitionSpec as P

NT = 768
LAGS = 1024
SRC = 128
CH_DEV = 16
CHANNELS = 512
BIN_DEV = 32
BINS = 512
PAIRS = 1024
NFFT = 1536
PARTS = 8
SLOTS = NFFT // 8 // PARTS
USED = 4 * SLOTS
CUTS = 4
LANES = 128
WIDE = 2 * LANES

bf16 = jnp.bfloat16
f32 = jnp.float32
dot = functools.partial(jnp.dot, preferred_element_type=f32)
HBM = pl.BlockSpec(memory_space=pltpu.MemorySpace.HBM)
VMEM = pl.BlockSpec(memory_space=pltpu.VMEM)
SMEM = pl.BlockSpec(memory_space=pltpu.SMEM)


def iota(shape, axis):
    return lax.broadcasted_iota(jnp.int32, shape, axis)


def angles(left, right):
    return (np.outer(left, right) % (2 * NFFT)) * (np.pi / NFFT)


def two_parts(exact):
    high = exact.astype(bf16)
    return np.stack([high, (exact - high.astype(np.float64)).astype(bf16)])


def forward_table():
    phase = angles(np.arange(NT), 2 * np.arange(NFFT // 8) + 1)
    return two_parts(np.concatenate([np.cos(phase), np.sin(phase)], axis=1))


def inverse_tables():
    lag = np.arange(LAGS) - LAGS // 2
    phase = angles(2 * np.arange(SLOTS) + 1, lag)
    turn = angles(np.arange(PARTS) * 2 * SLOTS, lag)
    scale = 2.0 / (NFFT * NT)
    turns = scale * np.stack([np.cos(turn), np.sin(turn)], axis=1)
    return two_parts(np.concatenate([np.cos(phase), np.sin(phase)], axis=0)), turns.astype(np.float32)


def spectra_kernel(records_hbm, table_hbm, rows_hbm, bins_hbm, places_hbm, out_ref, *scratch):
    *refs, sems = scratch
    rows_ref, bins_ref, places_ref, records_ref, table_ref = refs
    ends = [(rows_hbm, rows_ref), (bins_hbm, bins_ref), (places_hbm, places_ref), (records_hbm, records_ref)]
    for i in range(CUTS):
        cut = pl.ds(i * NT // CUTS, NT // CUTS)
        ends.append((table_hbm.at[:, cut, :], table_ref.at[:, cut, :]))
    copies = [pltpu.make_async_copy(source, target, sems.at[i]) for i, (source, target) in enumerate(ends)]
    for copy in copies:
        copy.start()
    for copy in copies[:3]:
        copy.wait()

    place = places_ref[...]
    owner, slot = place // BIN_DEV, place % BIN_DEV
    order = (slot // 8) * 128 + (owner // 4) * 32 + (owner % 2) * 16
    order = order + (slot % 4) * 4 + ((owner // 2) % 2) * 2 + (slot // 4) % 2
    digits = jnp.broadcast_to(order - BINS // 2, (8, BINS)).astype(f32).astype(bf16)
    bins = jnp.concatenate([bins_ref[0:1, :], bins_ref[1:2, :]], axis=1)
    spots = dot(digits, (iota((BINS, PAIRS), 0) == bins).astype(f32).astype(bf16))[0:1]
    rows = jnp.concatenate([rows_ref[0:1, :], rows_ref[1:2, :]], axis=1)

    chosen = iota((PAIRS // 16, PAIRS), 0) == iota((PAIRS // 16, PAIRS), 1) // 16

    def spread(values, first_lane):
        kept = jnp.where(chosen, values, 0.0).astype(bf16)
        lane = (iota((PAIRS, LANES), 0) % 16 + first_lane == iota((PAIRS, LANES), 1)).astype(f32).astype(bf16)
        return dot(kept, lane)

    lists_1 = spread((rows // SRC).astype(f32), USED) + spread((rows % SRC).astype(f32), USED + 16)
    lists_2 = spread(spots, USED)

    copies[3].wait()
    values = records_ref[...].astype(f32)
    mean_square = jnp.mean(values * values, axis=-1, keepdims=True)
    normed = values * lax.rsqrt(mean_square + 1e-06)
    turn = iota(normed.shape, 1) % 4
    split = jnp.concatenate([jnp.where(turn == k, normed, 0.0) for k in range(4)], axis=0).astype(bf16)
    for copy in copies[4:]:
        copy.wait()
    sums = dot(split, table_ref[0]) + dot(split, table_ref[1])
    half = PARTS * SLOTS
    c0, c1, c2, c3 = (sums[CH_DEV * k : CH_DEV * (k + 1), :half] for k in range(4))
    s0, s1, s2, s3 = (sums[CH_DEV * k : CH_DEV * (k + 1), half:] for k in range(4))
    cosines = (c0 + c2 + c1 + c3, c0 + c2 - c1 - c3, c0 - c2 - s1 + s3, c0 - c2 + s1 - s3)
    sines = (s0 + s2 + s1 + s3, s0 + s2 - s1 - s3, s0 - s2 + c1 - c3, s0 - s2 - c1 + c3)
    gap = jnp.zeros((CH_DEV, LANES - USED), f32)
    for z in range(PARTS):
        cut = slice(SLOTS * z, SLOTS * (z + 1))
        parts = [jnp.concatenate([item[:, cut] for item in items] + [gap], axis=1) for items in (cosines, sines)]
        for x in range(4):
            rows_x = slice(CH_DEV * x, CH_DEV * (x + 1))
            full = jnp.concatenate([parts[0] + lists_1[rows_x], parts[1] + lists_2[rows_x]], axis=1)
            out_ref[PARTS * x + z] = full.astype(bf16)


def make_spectra(records, rows, bins, places):
    table = jnp.asarray(forward_table())
    inputs = (rows, bins, places, records, table)
    return pl.pallas_call(
        spectra_kernel,
        out_shape=jax.ShapeDtypeStruct((4 * PARTS, CH_DEV, WIDE), bf16),
        in_specs=[HBM] * 5,
        out_specs=VMEM,
        scratch_shapes=[pltpu.VMEM(item.shape, item.dtype) for item in inputs] + [
            pltpu.SemaphoreType.DMA((4 + CUTS,))
        ],
        name="spectra",
    )(records, table, rows, bins, places)


def pairs_kernel(step_ref, given_ref, ids_ref, out_ref, src_ref, total_ref):
    ids = jnp.broadcast_to(ids_ref[pl.ds(step_ref[0], 1), :].astype(f32), (8, SRC)).T
    pick = (ids[:, 0:1] == iota((SRC, CHANNELS), 1).astype(f32)).astype(f32).astype(bf16)
    used = iota((SRC, WIDE), 1) % LANES < USED
    src_ref[...] = jnp.where(used, dot(pick, given_ref[...]), 0.0).astype(bf16)
    src_lane = iota((256, SRC), 1).astype(f32)
    recv_lane = (iota((256, 256), 1) - iota((256, 256), 0) // CH_DEV * CH_DEV).astype(f32)
    bin_row = (iota((BINS, 256), 0) - BINS // 2).astype(f32).astype(bf16)
    one, zero = jnp.ones((BINS, 256), bf16), jnp.zeros((BINS, 256), bf16)
    for half in range(2):
        block = slice(256 * half, 256 * (half + 1))
        columns = given_ref[block, :LANES].astype(f32)
        spots = given_ref[block, LANES:].astype(f32).T
        for group in range(4):
            products, matches = [], []
            for j in range(4 * group, 4 * group + 4):
                pick_r = (columns[:, USED + j : USED + j + 1] == recv_lane).astype(f32).astype(bf16)
                pick_s = (columns[:, USED + 16 + j : USED + 17 + j] == src_lane).astype(f32).astype(bf16)
                r, s = dot(pick_r, given_ref[block, :]), dot(pick_s, src_ref[...])
                rc, rs, sc, ss = r[:, :LANES], r[:, LANES:], s[:, :LANES], s[:, LANES:]
                product = jnp.concatenate([rc * sc + rs * ss, rs * sc - rc * ss], axis=1)
                products.append(product.astype(bf16))
                matches.append(jnp.where(bin_row == spots[USED + j : USED + j + 1, :].astype(bf16), one, zero))
            part = dot(jnp.concatenate(matches, axis=1), jnp.concatenate(products, axis=0))
            if half == 0 and group == 0:
                total_ref[...] = part
            elif half == 1 and group == 3:
                out_ref[...] = (total_ref[...] + part).astype(bf16)
            else:
                total_ref[...] += part


def bin_pairs(given, ids):
    step = (lax.axis_index("x") // 2).astype(jnp.int32).reshape(1)
    return pl.pallas_call(
        pairs_kernel,
        out_shape=jax.ShapeDtypeStruct((BINS, WIDE), bf16),
        in_specs=[SMEM, VMEM, VMEM],
        out_specs=VMEM,
        scratch_shapes=[pltpu.VMEM((SRC, WIDE), bf16), pltpu.VMEM((BINS, WIDE), f32)],
        compiler_params=pltpu.CompilerParams(vmem_limit_bytes=32 << 20),
        name="bin_pairs",
    )(step, given, ids)


def inverse_kernel(part_ref, parts_ref, base_ref, turns_ref, out_ref):
    spectrum = jnp.sum(parts_ref[...].astype(f32), axis=0)
    high = spectrum.astype(bf16)
    low = (spectrum - high.astype(f32)).astype(bf16)
    both = jnp.concatenate([high, low], axis=0)
    count = high.shape[0]
    turn = iota((1, LAGS), 1) % 4
    sign = (1 - 2 * (turn % 2)).astype(f32)
    even = jnp.where(turn == 0, 1.0, jnp.where(turn == 2, -1.0, 0.0))
    odd = jnp.where(turn == 1, 1.0, jnp.where(turn == 3, -1.0, 0.0))
    gap = jnp.zeros((LANES - USED, LAGS), f32)
    real, imag = 0.0, 0.0
    for i, left in enumerate((both, high)):
        cos, sin = base_ref[i, :SLOTS, :].astype(f32), base_ref[i, SLOTS:, :].astype(f32)
        coses = [cos, sign * cos, even * cos - odd * sin, even * cos + odd * sin, gap]
        sines = [sin, sign * sin, even * sin + odd * cos, even * sin - odd * cos, gap]
        for_real = jnp.concatenate(coses + [-item for item in sines], axis=0).astype(bf16)
        for_imag = jnp.concatenate(sines + coses, axis=0).astype(bf16)
        a, b = dot(left, for_real), dot(left, for_imag)
        real, imag = real + a[:count], imag + b[:count]
        if i == 0:
            real, imag = real + a[count:], imag + b[count:]
    turns = turns_ref[part_ref[0]]
    lags = real * turns[0:1] - imag * turns[1:2]
    for group in range(8):
        tile = lags[:, LANES * group : LANES * (group + 1)]
        for quarter in range(4):
            lane = slice(32 * quarter, 32 * (quarter + 1))
            out_ref[4 * group + quarter] = jnp.concatenate([tile[4 * c : 4 * c + 4, lane] for c in range(4)], axis=1)


def invert(parts):
    base, turns = inverse_tables()
    part = lax.axis_index("zl").astype(jnp.int32).reshape(1)
    return pl.pallas_call(
        inverse_kernel,
        out_shape=jax.ShapeDtypeStruct((32, 4, LANES), f32),
        in_specs=[SMEM, VMEM, VMEM, VMEM],
        out_specs=VMEM,
        compiler_params=pltpu.CompilerParams(vmem_limit_bytes=32 << 20),
        name="invert",
    )(part, parts, jnp.asarray(base), jnp.asarray(turns))


def exchange(value, axes):
    return lax.all_to_all(value, axes, split_axis=0, concat_axis=0, tiled=True)


def shards(records, source_ids, pair_rows, pair_bins, bin_places):
    spectra = make_spectra(records.reshape(CH_DEV, NT), pair_rows, pair_bins, bin_places.reshape(1, BINS))
    given = exchange(spectra, ("x", "zl")).reshape(CHANNELS, WIDE)
    parts = exchange(bin_pairs(given, source_ids).reshape(32, 16, WIDE), ("x", "y", "core"))
    shares = exchange(invert(parts).reshape(64, 2, LANES), ("x", "zl", "zh"))
    return jnp.sum(shares.reshape(4, 16, 2, LANES), axis=1).reshape(BIN_DEV, 32)


def solution(mesh):
    fine = Mesh(mesh.devices.reshape(4, 8, 4, 2, 2), ("x", "zl", "y", "zh", "core"))
    chan, tm = ("x", "zl"), ("y", "zh", "core")
    in_specs = (P(chan, tm, None), P(), P(None, chan), P(None, chan), P())
    return jax.shard_map(shards, mesh=fine, in_specs=in_specs, out_specs=P(tm, chan), check_vma=False)
```

```python
import functools

import jax
import jax.numpy as jnp
import numpy as np
from jax import lax
from jax.experimental import pallas as pl
from jax.experimental.pallas import tpu as pltpu
from jax.sharding import Mesh, PartitionSpec as P

NT = 768
LAGS = 1024
SRC = 128
CH_DEV = 16
CHANNELS = 512
BIN_DEV = 32
BINS = 512
PAIRS = 1024
NFFT = 1536
PARTS = 8
SLOTS = NFFT // 8 // PARTS
USED = 4 * SLOTS
CUTS = 4
LANES = 128
WIDE = 2 * LANES

bf16 = jnp.bfloat16
f32 = jnp.float32
dot = functools.partial(jnp.dot, preferred_element_type=f32)
HBM = pl.BlockSpec(memory_space=pltpu.MemorySpace.HBM)
VMEM = pl.BlockSpec(memory_space=pltpu.VMEM)


def iota(shape, axis):
    return lax.broadcasted_iota(jnp.int32, shape, axis)


def angles(left, right):
    return (np.outer(left, right) % (2 * NFFT)) * (np.pi / NFFT)


def two_parts(exact):
    high = exact.astype(bf16)
    return np.stack([high, (exact - high.astype(np.float64)).astype(bf16)])


def forward_table():
    phase = angles(np.arange(NT), 2 * np.arange(NFFT // 8) + 1)
    return two_parts(np.concatenate([np.cos(phase), np.sin(phase)], axis=1))


def inverse_tables():
    lag = np.arange(LAGS) - LAGS // 2
    phase = angles(2 * np.arange(SLOTS) + 1, lag)
    turn = angles(np.arange(PARTS) * 2 * SLOTS, lag)
    scale = 2.0 / (NFFT * NT)
    turns = scale * np.stack([np.cos(turn), np.sin(turn)], axis=1)
    return two_parts(np.concatenate([np.cos(phase), np.sin(phase)], axis=0)), turns.astype(np.float32)


def spectra_kernel(records_hbm, table_hbm, rows_hbm, bins_hbm, places_hbm, out_ref, *scratch):
    *refs, sems = scratch
    rows_ref, bins_ref, places_ref, records_ref, table_ref = refs
    ends = [(rows_hbm, rows_ref), (bins_hbm, bins_ref), (places_hbm, places_ref), (records_hbm, records_ref)]
    for i in range(CUTS):
        cut = pl.ds(i * NT // CUTS, NT // CUTS)
        ends.append((table_hbm.at[:, cut, :], table_ref.at[:, cut, :]))
    copies = [pltpu.make_async_copy(source, target, sems.at[i]) for i, (source, target) in enumerate(ends)]
    for copy in copies:
        copy.start()
    for copy in copies[:3]:
        copy.wait()

    place = places_ref[...]
    owner, slot = place // BIN_DEV, place % BIN_DEV
    order = (slot // 8) * 128 + (owner // 4) * 32 + (owner % 2) * 16
    order = order + (slot % 4) * 4 + ((owner // 2) % 2) * 2 + (slot // 4) % 2
    digits = jnp.broadcast_to(order - BINS // 2, (8, BINS)).astype(f32).astype(bf16)
    bins = jnp.concatenate([bins_ref[0:1, :], bins_ref[1:2, :]], axis=1)
    spots = dot(digits, (iota((BINS, PAIRS), 0) == bins).astype(f32).astype(bf16))[0:1]
    rows = jnp.concatenate([rows_ref[0:1, :], rows_ref[1:2, :]], axis=1)

    chosen = iota((PAIRS // 16, PAIRS), 0) == iota((PAIRS // 16, PAIRS), 1) // 16

    def spread(values, first_lane):
        kept = jnp.where(chosen, values, 0.0).astype(bf16)
        lane = (iota((PAIRS, LANES), 0) % 16 + first_lane == iota((PAIRS, LANES), 1)).astype(f32).astype(bf16)
        return dot(kept, lane)

    lists_1 = spread((rows // SRC).astype(f32), USED) + spread((rows % SRC).astype(f32), USED + 16)
    lists_2 = spread(spots, USED)

    copies[3].wait()
    values = records_ref[...].astype(f32)
    mean_square = jnp.mean(values * values, axis=-1, keepdims=True)
    normed = values * lax.rsqrt(mean_square + 1e-06)
    turn = iota(normed.shape, 1) % 4
    split = jnp.concatenate([jnp.where(turn == k, normed, 0.0) for k in range(4)], axis=0).astype(bf16)
    for copy in copies[4:]:
        copy.wait()
    sums = dot(split, table_ref[0]) + dot(split, table_ref[1])
    half = PARTS * SLOTS
    c0, c1, c2, c3 = (sums[CH_DEV * k : CH_DEV * (k + 1), :half] for k in range(4))
    s0, s1, s2, s3 = (sums[CH_DEV * k : CH_DEV * (k + 1), half:] for k in range(4))
    cosines = (c0 + c2 + c1 + c3, c0 + c2 - c1 - c3, c0 - c2 - s1 + s3, c0 - c2 + s1 - s3)
    sines = (s0 + s2 + s1 + s3, s0 + s2 - s1 - s3, s0 - s2 + c1 - c3, s0 - s2 - c1 + c3)
    gap = jnp.zeros((CH_DEV, LANES - USED), f32)
    for z in range(PARTS):
        cut = slice(SLOTS * z, SLOTS * (z + 1))
        parts = [jnp.concatenate([item[:, cut] for item in items] + [gap], axis=1) for items in (cosines, sines)]
        for x in range(4):
            rows_x = slice(CH_DEV * x, CH_DEV * (x + 1))
            full = jnp.concatenate([parts[0] + lists_1[rows_x], parts[1] + lists_2[rows_x]], axis=1)
            out_ref[PARTS * x + z] = full.astype(bf16)


def make_spectra(records, rows, bins, places):
    table = jnp.asarray(forward_table())
    inputs = (rows, bins, places, records, table)
    rows, bins, places, records, table = (pltpu.with_memory_space_constraint(item, pltpu.HBM) for item in inputs)
    return pl.pallas_call(
        spectra_kernel,
        out_shape=jax.ShapeDtypeStruct((4 * PARTS, CH_DEV, WIDE), bf16),
        in_specs=[HBM] * 5,
        out_specs=VMEM,
        scratch_shapes=[pltpu.VMEM(item.shape, item.dtype) for item in inputs] + [
            pltpu.SemaphoreType.DMA((4 + CUTS,))
        ],
        compiler_params=pltpu.CompilerParams(vmem_limit_bytes=16 << 20),
        name="spectra",
    )(records, table, rows, bins, places)


def pairs_kernel(given_ref, ids_ref, out_ref, src_ref, total_ref):
    ids = jnp.broadcast_to(ids_ref[pl.ds(lax.axis_index("x") // 2, 1), :].astype(f32), (8, SRC)).T
    pick = (ids[:, 0:1] == iota((SRC, CHANNELS), 1).astype(f32)).astype(f32).astype(bf16)
    used = iota((SRC, WIDE), 1) % LANES < USED
    src_ref[...] = jnp.where(used, dot(pick, given_ref[...]), 0.0).astype(bf16)
    src_lane = iota((256, SRC), 1).astype(f32)
    recv_lane = (iota((256, 256), 1) - iota((256, 256), 0) // CH_DEV * CH_DEV).astype(f32)
    bin_row = (iota((BINS, 256), 0) - BINS // 2).astype(f32).astype(bf16)
    one, zero = jnp.ones((BINS, 256), bf16), jnp.zeros((BINS, 256), bf16)
    for half in range(2):
        block = slice(256 * half, 256 * (half + 1))
        columns = given_ref[block, :LANES].astype(f32)
        spots = given_ref[block, LANES:].astype(f32).T
        for group in range(4):
            products, matches = [], []
            for j in range(4 * group, 4 * group + 4):
                pick_r = (columns[:, USED + j : USED + j + 1] == recv_lane).astype(f32).astype(bf16)
                pick_s = (columns[:, USED + 16 + j : USED + 17 + j] == src_lane).astype(f32).astype(bf16)
                r, s = dot(pick_r, given_ref[block, :]), dot(pick_s, src_ref[...])
                rc, rs, sc, ss = r[:, :LANES], r[:, LANES:], s[:, :LANES], s[:, LANES:]
                product = jnp.concatenate([rc * sc + rs * ss, rs * sc - rc * ss], axis=1)
                products.append(product.astype(bf16))
                matches.append(jnp.where(bin_row == spots[USED + j : USED + j + 1, :].astype(bf16), one, zero))
            part = dot(jnp.concatenate(matches, axis=1), jnp.concatenate(products, axis=0))
            if half == 0 and group == 0:
                total_ref[...] = part
            elif half == 1 and group == 3:
                out_ref[...] = (total_ref[...] + part).astype(bf16)
            else:
                total_ref[...] += part


def bin_pairs(given, ids):
    return pl.pallas_call(
        pairs_kernel,
        out_shape=jax.ShapeDtypeStruct((BINS, WIDE), bf16),
        in_specs=[VMEM, VMEM],
        out_specs=VMEM,
        scratch_shapes=[pltpu.VMEM((SRC, WIDE), bf16), pltpu.VMEM((BINS, WIDE), f32)],
        compiler_params=pltpu.CompilerParams(vmem_limit_bytes=32 << 20),
        name="bin_pairs",
    )(given, ids)


def inverse_kernel(parts_ref, base_ref, turns_ref, out_ref):
    spectrum = jnp.sum(parts_ref[...].astype(f32), axis=0)
    high = spectrum.astype(bf16)
    low = (spectrum - high.astype(f32)).astype(bf16)
    both = jnp.concatenate([high, low], axis=0)
    count = high.shape[0]
    turn = iota((1, LAGS), 1) % 4
    sign = (1 - 2 * (turn % 2)).astype(f32)
    even = jnp.where(turn == 0, 1.0, jnp.where(turn == 2, -1.0, 0.0))
    odd = jnp.where(turn == 1, 1.0, jnp.where(turn == 3, -1.0, 0.0))
    gap = jnp.zeros((LANES - USED, LAGS), f32)
    real, imag = 0.0, 0.0
    for i, left in enumerate((both, high)):
        cos, sin = base_ref[i, :SLOTS, :].astype(f32), base_ref[i, SLOTS:, :].astype(f32)
        coses = [cos, sign * cos, even * cos - odd * sin, even * cos + odd * sin, gap]
        sines = [sin, sign * sin, even * sin + odd * cos, even * sin - odd * cos, gap]
        for_real = jnp.concatenate(coses + [-item for item in sines], axis=0).astype(bf16)
        for_imag = jnp.concatenate(sines + coses, axis=0).astype(bf16)
        a, b = dot(left, for_real), dot(left, for_imag)
        real, imag = real + a[:count], imag + b[:count]
        if i == 0:
            real, imag = real + a[count:], imag + b[count:]
    turns = turns_ref[lax.axis_index("zl")]
    lags = real * turns[0:1] - imag * turns[1:2]
    for group in range(8):
        tile = lags[:, LANES * group : LANES * (group + 1)]
        for quarter in range(4):
            lane = slice(32 * quarter, 32 * (quarter + 1))
            out_ref[4 * group + quarter] = jnp.concatenate([tile[4 * c : 4 * c + 4, lane] for c in range(4)], axis=1)


def invert(parts):
    base, turns = inverse_tables()
    return pl.pallas_call(
        inverse_kernel,
        out_shape=jax.ShapeDtypeStruct((32, 4, LANES), f32),
        in_specs=[VMEM, VMEM, VMEM],
        out_specs=VMEM,
        compiler_params=pltpu.CompilerParams(vmem_limit_bytes=32 << 20),
        name="invert",
    )(parts, jnp.asarray(base), jnp.asarray(turns))


def exchange(value, axes):
    return lax.all_to_all(value, axes, split_axis=0, concat_axis=0, tiled=True)


def shards(records, source_ids, pair_rows, pair_bins, bin_places):
    spectra = make_spectra(records.reshape(CH_DEV, NT), pair_rows, pair_bins, bin_places.reshape(1, BINS))
    given = exchange(spectra, ("x", "zl")).reshape(CHANNELS, WIDE)
    parts = exchange(bin_pairs(given, source_ids).reshape(32, 16, WIDE), ("x", "y", "core"))
    shares = exchange(invert(parts).reshape(64, 2, LANES), ("x", "zl", "zh"))
    return jnp.sum(shares.reshape(4, 16, 2, LANES), axis=1).reshape(BIN_DEV, 32)


def solution(mesh):
    fine = Mesh(mesh.devices.reshape(4, 8, 4, 2, 2), ("x", "zl", "y", "zh", "core"))
    chan, tm = ("x", "zl"), ("y", "zh", "core")
    in_specs = (P(chan, tm, None), P(), P(None, chan), P(None, chan), P())
    return jax.shard_map(shards, mesh=fine, in_specs=in_specs, out_specs=P(tm, chan), check_vma=False)
```

```python
import functools

import jax
import jax.numpy as jnp
import numpy as np
from jax import lax
from jax.experimental import pallas as pl
from jax.experimental.pallas import tpu as pltpu
from jax.sharding import Mesh, PartitionSpec as P

NT = 768
LAGS = 1024
SRC = 128
CH_DEV = 16
CHANNELS = 512
BIN_DEV = 32
BINS = 512
PAIRS = 1024
NFFT = 1536
PARTS = 8
SLOTS = NFFT // 8 // PARTS
USED = 4 * SLOTS
CUTS = 4
LANES = 128
WIDE = 2 * LANES

bf16 = jnp.bfloat16
f32 = jnp.float32
dot = functools.partial(jnp.dot, preferred_element_type=f32)
HBM = pl.BlockSpec(memory_space=pltpu.MemorySpace.HBM)
VMEM = pl.BlockSpec(memory_space=pltpu.VMEM)


def iota(shape, axis):
    return lax.broadcasted_iota(jnp.int32, shape, axis)


def angles(left, right):
    return (np.outer(left, right) % (2 * NFFT)) * (np.pi / NFFT)


def two_parts(exact):
    high = exact.astype(bf16)
    return np.stack([high, (exact - high.astype(np.float64)).astype(bf16)])


def forward_table():
    phase = angles(np.arange(NT), 2 * np.arange(NFFT // 8) + 1)
    return two_parts(np.concatenate([np.cos(phase), np.sin(phase)], axis=1))


def inverse_tables():
    lag = np.arange(LAGS) - LAGS // 2
    phase = angles(2 * np.arange(SLOTS) + 1, lag)
    turn = angles(np.arange(PARTS) * 2 * SLOTS, lag)
    scale = 2.0 / (NFFT * NT)
    turns = scale * np.stack([np.cos(turn), np.sin(turn)], axis=1)
    return two_parts(np.concatenate([np.cos(phase), np.sin(phase)], axis=0)), turns.astype(np.float32)


def spectra_kernel(records_hbm, table_hbm, rows_hbm, bins_hbm, places_hbm, out_ref, *scratch):
    *refs, sems = scratch
    rows_ref, bins_ref, places_ref, records_ref, table_ref = refs
    ends = [(rows_hbm, rows_ref), (bins_hbm, bins_ref), (places_hbm, places_ref), (records_hbm, records_ref)]
    for i in range(CUTS):
        cut = pl.ds(i * NT // CUTS, NT // CUTS)
        ends.append((table_hbm.at[:, cut, :], table_ref.at[:, cut, :]))
    copies = [pltpu.make_async_copy(source, target, sems.at[i]) for i, (source, target) in enumerate(ends)]
    for copy in copies:
        copy.start()
    for copy in copies[:3]:
        copy.wait()

    place = places_ref[...]
    owner, slot = place // BIN_DEV, place % BIN_DEV
    order = (owner // 4) * 128 + (owner % 2) * 64 + ((owner // 2) % 2) * 32 + (slot % 4) * 8 + slot // 4
    digits = jnp.broadcast_to(order - BINS // 2, (8, BINS)).astype(f32).astype(bf16)
    bins = jnp.concatenate([bins_ref[0:1, :], bins_ref[1:2, :]], axis=1)
    spots = dot(digits, (iota((BINS, PAIRS), 0) == bins).astype(f32).astype(bf16))[0:1]
    rows = jnp.concatenate([rows_ref[0:1, :], rows_ref[1:2, :]], axis=1)

    chosen = iota((PAIRS // 16, PAIRS), 0) == iota((PAIRS // 16, PAIRS), 1) // 16

    def spread(values, first_lane):
        kept = jnp.where(chosen, values, 0.0).astype(bf16)
        lane = (iota((PAIRS, LANES), 0) % 16 + first_lane == iota((PAIRS, LANES), 1)).astype(f32).astype(bf16)
        return dot(kept, lane)

    lists_1 = spread((rows // SRC).astype(f32), USED) + spread((rows % SRC).astype(f32), USED + 16)
    lists_2 = spread(spots, USED)

    copies[3].wait()
    values = records_ref[...].astype(f32)
    mean_square = jnp.mean(values * values, axis=-1, keepdims=True)
    normed = values * lax.rsqrt(mean_square + 1e-06)
    turn = iota(normed.shape, 1) % 4
    split = jnp.concatenate([jnp.where(turn == k, normed, 0.0) for k in range(4)], axis=0).astype(bf16)
    for copy in copies[4:]:
        copy.wait()
    sums = dot(split, table_ref[0]) + dot(split, table_ref[1])
    half = PARTS * SLOTS
    c0, c1, c2, c3 = (sums[CH_DEV * k : CH_DEV * (k + 1), :half] for k in range(4))
    s0, s1, s2, s3 = (sums[CH_DEV * k : CH_DEV * (k + 1), half:] for k in range(4))
    cosines = (c0 + c2 + c1 + c3, c0 + c2 - c1 - c3, c0 - c2 - s1 + s3, c0 - c2 + s1 - s3)
    sines = (s0 + s2 + s1 + s3, s0 + s2 - s1 - s3, s0 - s2 + c1 - c3, s0 - s2 - c1 + c3)
    gap = jnp.zeros((CH_DEV, LANES - USED), f32)
    for z in range(PARTS):
        cut = slice(SLOTS * z, SLOTS * (z + 1))
        parts = [jnp.concatenate([item[:, cut] for item in items] + [gap], axis=1) for items in (cosines, sines)]
        for x in range(4):
            rows_x = slice(CH_DEV * x, CH_DEV * (x + 1))
            full = jnp.concatenate([parts[0] + lists_1[rows_x], parts[1] + lists_2[rows_x]], axis=1)
            out_ref[PARTS * x + z] = full.astype(bf16)


def make_spectra(records, rows, bins, places):
    table = jnp.asarray(forward_table())
    inputs = (rows, bins, places, records, table)
    rows, bins, places, records, table = (pltpu.with_memory_space_constraint(item, pltpu.HBM) for item in inputs)
    return pl.pallas_call(
        spectra_kernel,
        out_shape=jax.ShapeDtypeStruct((4 * PARTS, CH_DEV, WIDE), bf16),
        in_specs=[HBM] * 5,
        out_specs=VMEM,
        scratch_shapes=[pltpu.VMEM(item.shape, item.dtype) for item in inputs] + [
            pltpu.SemaphoreType.DMA((4 + CUTS,))
        ],
        compiler_params=pltpu.CompilerParams(vmem_limit_bytes=16 << 20),
        name="spectra",
    )(records, table, rows, bins, places)


def pack(total, out_ref):
    for i in range(8):
        kept, moved = total[64 * i : 64 * i + 48], total[64 * i + 48 : 64 * i + 64]
        tiles = []
        for start in (0, LANES):
            thirds = [moved[:, start + 32 * k : start + 32 * (k + 1)] for k in range(3)]
            tiles += [kept[:, start : start + USED], jnp.concatenate(thirds, axis=0)]
        out_ref[i] = jnp.concatenate(tiles, axis=1).astype(bf16)


def unpack(packed):
    moved = []
    for start in (0, LANES):
        spare = packed[:, start + USED : start + LANES]
        thirds = [spare[16 * k : 16 * (k + 1)] for k in range(3)]
        moved += thirds + [jnp.zeros((16, LANES - USED), f32)]
    return jnp.concatenate([packed, jnp.concatenate(moved, axis=1)], axis=0)


def pairs_kernel(given_ref, ids_ref, out_ref, src_ref, total_ref):
    ids = jnp.broadcast_to(ids_ref[pl.ds(lax.axis_index("x") // 2, 1), :].astype(f32), (8, SRC)).T
    pick = (ids[:, 0:1] == iota((SRC, CHANNELS), 1).astype(f32)).astype(f32).astype(bf16)
    used = iota((SRC, WIDE), 1) % LANES < USED
    src_ref[...] = jnp.where(used, dot(pick, given_ref[...]), 0.0).astype(bf16)
    src_lane = iota((256, SRC), 1).astype(f32)
    recv_lane = (iota((256, 256), 1) - iota((256, 256), 0) // CH_DEV * CH_DEV).astype(f32)
    bin_row = (iota((BINS, 256), 0) - BINS // 2).astype(f32).astype(bf16)
    one, zero = jnp.ones((BINS, 256), bf16), jnp.zeros((BINS, 256), bf16)
    for half in range(2):
        block = slice(256 * half, 256 * (half + 1))
        columns = given_ref[block, :LANES].astype(f32)
        spots = given_ref[block, LANES:].astype(f32).T
        for group in range(4):
            products, matches = [], []
            for j in range(4 * group, 4 * group + 4):
                pick_r = (columns[:, USED + j : USED + j + 1] == recv_lane).astype(f32).astype(bf16)
                pick_s = (columns[:, USED + 16 + j : USED + 17 + j] == src_lane).astype(f32).astype(bf16)
                r, s = dot(pick_r, given_ref[block, :]), dot(pick_s, src_ref[...])
                rc, rs, sc, ss = r[:, :LANES], r[:, LANES:], s[:, :LANES], s[:, LANES:]
                product = jnp.concatenate([rc * sc + rs * ss, rs * sc - rc * ss], axis=1)
                products.append(product.astype(bf16))
                matches.append(jnp.where(bin_row == spots[USED + j : USED + j + 1, :].astype(bf16), one, zero))
            part = dot(jnp.concatenate(matches, axis=1), jnp.concatenate(products, axis=0))
            if half == 0 and group == 0:
                total_ref[...] = part
            elif half == 1 and group == 3:
                pack(total_ref[...] + part, out_ref)
            else:
                total_ref[...] += part


def bin_pairs(given, ids):
    return pl.pallas_call(
        pairs_kernel,
        out_shape=jax.ShapeDtypeStruct((8, 48, WIDE), bf16),
        in_specs=[VMEM, VMEM],
        out_specs=VMEM,
        scratch_shapes=[pltpu.VMEM((SRC, WIDE), bf16), pltpu.VMEM((BINS, WIDE), f32)],
        compiler_params=pltpu.CompilerParams(vmem_limit_bytes=32 << 20),
        name="bin_pairs",
    )(given, ids)


def inverse_kernel(parts_ref, base_ref, turns_ref, out_ref):
    spectrum = unpack(jnp.sum(parts_ref[...].astype(f32), axis=0))
    high = spectrum.astype(bf16)
    low = (spectrum - high.astype(f32)).astype(bf16)
    both = jnp.concatenate([high, low], axis=0)
    count = high.shape[0]
    turn = iota((1, LAGS), 1) % 4
    sign = (1 - 2 * (turn % 2)).astype(f32)
    even = jnp.where(turn == 0, 1.0, jnp.where(turn == 2, -1.0, 0.0))
    odd = jnp.where(turn == 1, 1.0, jnp.where(turn == 3, -1.0, 0.0))
    gap = jnp.zeros((LANES - USED, LAGS), f32)
    real, imag = 0.0, 0.0
    for i, left in enumerate((both, high)):
        cos, sin = base_ref[i, :SLOTS, :].astype(f32), base_ref[i, SLOTS:, :].astype(f32)
        coses = [cos, sign * cos, even * cos - odd * sin, even * cos + odd * sin, gap]
        sines = [sin, sign * sin, even * sin + odd * cos, even * sin - odd * cos, gap]
        for_real = jnp.concatenate(coses + [-item for item in sines], axis=0).astype(bf16)
        for_imag = jnp.concatenate(sines + coses, axis=0).astype(bf16)
        a, b = dot(left, for_real), dot(left, for_imag)
        real, imag = real + a[:count], imag + b[:count]
        if i == 0:
            real, imag = real + a[count:], imag + b[count:]
    turns = turns_ref[lax.axis_index("zl")]
    lags = real * turns[0:1] - imag * turns[1:2]
    for zh in range(2):
        for group in range(8):
            tile = lags[32 * zh : 32 * (zh + 1), LANES * group : LANES * (group + 1)]
            for quarter in range(4):
                lane = slice(32 * quarter, 32 * (quarter + 1))
                pieces = [tile[8 * c : 8 * c + 8, lane] for c in range(4)]
                out_ref[8 * group + 2 * quarter + zh] = jnp.concatenate(pieces, axis=1).astype(bf16)


def invert(parts):
    base, turns = inverse_tables()
    return pl.pallas_call(
        inverse_kernel,
        out_shape=jax.ShapeDtypeStruct((64, 8, LANES), bf16),
        in_specs=[VMEM, VMEM, VMEM],
        out_specs=VMEM,
        compiler_params=pltpu.CompilerParams(vmem_limit_bytes=32 << 20),
        name="invert",
    )(parts, jnp.asarray(base), jnp.asarray(turns))


def exchange(value, axes):
    return lax.all_to_all(value, axes, split_axis=0, concat_axis=0, tiled=True)


def shards(records, source_ids, pair_rows, pair_bins, bin_places):
    spectra = make_spectra(records.reshape(CH_DEV, NT), pair_rows, pair_bins, bin_places.reshape(1, BINS))
    given = exchange(spectra, ("x", "zl")).reshape(CHANNELS, WIDE)
    parts = exchange(bin_pairs(given, source_ids), ("y", "core"))
    shares = exchange(invert(parts), ("x", "zl", "zh"))
    return jnp.sum(shares.astype(f32), axis=0).reshape(BIN_DEV, 32)


def solution(mesh):
    fine = Mesh(mesh.devices.reshape(4, 8, 4, 2, 2), ("x", "zl", "y", "zh", "core"))
    chan, tm = ("x", "zl"), ("y", "zh", "core")
    in_specs = (P(chan, tm, None), P(), P(None, chan), P(None, chan), P())
    return jax.shard_map(shards, mesh=fine, in_specs=in_specs, out_specs=P(tm, chan), check_vma=False)
```

```python
import functools

import jax
import jax.numpy as jnp
import numpy as np
from jax import lax
from jax.experimental import pallas as pl
from jax.experimental.pallas import tpu as pltpu
from jax.sharding import Mesh, PartitionSpec as P

NT = 768
LAGS = 1024
SRC = 128
CH_DEV = 16
CHANNELS = 512
BIN_DEV = 32
BINS = 512
PAIRS = 1024
NFFT = 1536
PARTS = 8
SLOTS = NFFT // 8 // PARTS
USED = 4 * SLOTS
CUTS = 4
LANES = 128
WIDE = 2 * LANES

bf16 = jnp.bfloat16
f32 = jnp.float32
dot = functools.partial(jnp.dot, preferred_element_type=f32)
HBM = pl.BlockSpec(memory_space=pltpu.MemorySpace.HBM)
VMEM = pl.BlockSpec(memory_space=pltpu.VMEM)


def iota(shape, axis):
    return lax.broadcasted_iota(jnp.int32, shape, axis)


def angles(left, right):
    return (np.outer(left, right) % (2 * NFFT)) * (np.pi / NFFT)


def two_parts(exact):
    high = exact.astype(bf16)
    return np.stack([high, (exact - high.astype(np.float64)).astype(bf16)])


def forward_table():
    phase = angles(np.arange(NT), 2 * np.arange(NFFT // 8) + 1)
    return two_parts(np.concatenate([np.cos(phase), np.sin(phase)], axis=1))


def inverse_tables():
    lag = np.arange(LAGS) - LAGS // 2
    phase = angles(2 * np.arange(SLOTS) + 1, lag)
    turn = angles(np.arange(PARTS) * 2 * SLOTS, lag)
    scale = 2.0 / (NFFT * NT)
    turns = scale * np.stack([np.cos(turn), np.sin(turn)], axis=1)
    return two_parts(np.concatenate([np.cos(phase), np.sin(phase)], axis=0)), turns.astype(np.float32)


def spectra_kernel(records_hbm, table_hbm, rows_hbm, bins_hbm, places_hbm, out_ref, *scratch):
    *refs, sems = scratch
    rows_ref, bins_ref, places_ref, records_ref, table_ref = refs
    ends = [(rows_hbm, rows_ref), (bins_hbm, bins_ref), (places_hbm, places_ref), (records_hbm, records_ref)]
    for i in range(CUTS):
        cut = pl.ds(i * NT // CUTS, NT // CUTS)
        ends.append((table_hbm.at[:, cut, :], table_ref.at[:, cut, :]))
    copies = [pltpu.make_async_copy(source, target, sems.at[i]) for i, (source, target) in enumerate(ends)]
    for copy in copies:
        copy.start()
    for copy in copies[:3]:
        copy.wait()

    place = places_ref[...]
    owner, slot = place // BIN_DEV, place % BIN_DEV
    order = (owner // 4) * 128 + (owner % 2) * 64 + ((owner // 2) % 2) * 32 + (slot % 4) * 8 + slot // 4
    digits = jnp.broadcast_to(order - BINS // 2, (8, BINS)).astype(f32).astype(bf16)
    bins = jnp.concatenate([bins_ref[0:1, :], bins_ref[1:2, :]], axis=1)
    spots = dot(digits, (iota((BINS, PAIRS), 0) == bins).astype(f32).astype(bf16))[0:1]
    rows = jnp.concatenate([rows_ref[0:1, :], rows_ref[1:2, :]], axis=1)

    chosen = iota((PAIRS // 16, PAIRS), 0) == iota((PAIRS // 16, PAIRS), 1) // 16

    def spread(values, first_lane):
        kept = jnp.where(chosen, values, 0.0).astype(bf16)
        lane = (iota((PAIRS, LANES), 0) % 16 + first_lane == iota((PAIRS, LANES), 1)).astype(f32).astype(bf16)
        return dot(kept, lane)

    lists_1 = spread((rows // SRC).astype(f32), USED) + spread((rows % SRC).astype(f32), USED + 16)
    lists_2 = spread(spots, USED)

    copies[3].wait()
    values = records_ref[...].astype(f32)
    mean_square = jnp.mean(values * values, axis=-1, keepdims=True)
    normed = values * lax.rsqrt(mean_square + 1e-06)
    turn = iota(normed.shape, 1) % 4
    split = jnp.concatenate([jnp.where(turn == k, normed, 0.0) for k in range(4)], axis=0).astype(bf16)
    for copy in copies[4:]:
        copy.wait()
    sums = dot(split, table_ref[0]) + dot(split, table_ref[1])
    half = PARTS * SLOTS
    c0, c1, c2, c3 = (sums[CH_DEV * k : CH_DEV * (k + 1), :half] for k in range(4))
    s0, s1, s2, s3 = (sums[CH_DEV * k : CH_DEV * (k + 1), half:] for k in range(4))
    cosines = (c0 + c2 + c1 + c3, c0 + c2 - c1 - c3, c0 - c2 - s1 + s3, c0 - c2 + s1 - s3)
    sines = (s0 + s2 + s1 + s3, s0 + s2 - s1 - s3, s0 - s2 + c1 - c3, s0 - s2 - c1 + c3)
    gap = jnp.zeros((CH_DEV, LANES - USED), f32)
    for z in range(PARTS):
        cut = slice(SLOTS * z, SLOTS * (z + 1))
        parts = [jnp.concatenate([item[:, cut] for item in items] + [gap], axis=1) for items in (cosines, sines)]
        for x in range(4):
            rows_x = slice(CH_DEV * x, CH_DEV * (x + 1))
            full = jnp.concatenate([parts[0] + lists_1[rows_x], parts[1] + lists_2[rows_x]], axis=1)
            out_ref[4 * z + x] = full.astype(bf16)


def make_spectra(records, rows, bins, places):
    table = jnp.asarray(forward_table())
    inputs = (rows, bins, places, records, table)
    rows, bins, places, records, table = (pltpu.with_memory_space_constraint(item, pltpu.HBM) for item in inputs)
    return pl.pallas_call(
        spectra_kernel,
        out_shape=jax.ShapeDtypeStruct((4 * PARTS, CH_DEV, WIDE), bf16),
        in_specs=[HBM] * 5,
        out_specs=VMEM,
        scratch_shapes=[pltpu.VMEM(item.shape, item.dtype) for item in inputs] + [
            pltpu.SemaphoreType.DMA((4 + CUTS,))
        ],
        compiler_params=pltpu.CompilerParams(vmem_limit_bytes=16 << 20),
        name="spectra",
    )(records, table, rows, bins, places)


def pack(total, out_ref):
    for i in range(8):
        kept, moved = total[64 * i : 64 * i + 48], total[64 * i + 48 : 64 * i + 64]
        tiles = []
        for start in (0, LANES):
            thirds = [moved[:, start + 32 * k : start + 32 * (k + 1)] for k in range(3)]
            tiles += [kept[:, start : start + USED], jnp.concatenate(thirds, axis=0)]
        out_ref[i] = jnp.concatenate(tiles, axis=1).astype(bf16)


def unpack(packed):
    moved = []
    for start in (0, LANES):
        spare = packed[:, start + USED : start + LANES]
        thirds = [spare[16 * k : 16 * (k + 1)] for k in range(3)]
        moved += thirds + [jnp.zeros((16, LANES - USED), f32)]
    return jnp.concatenate([packed, jnp.concatenate(moved, axis=1)], axis=0)


def pairs_kernel(given_ref, ids_ref, out_ref, src_ref, total_ref):
    ids = ids_ref[pl.ds(lax.axis_index("x") // 2, 1), :]
    block = ids // CH_DEV
    ids = (block % PARTS * 4 + block // PARTS) * CH_DEV + ids % CH_DEV
    ids = jnp.broadcast_to(ids.astype(f32), (8, SRC)).T
    pick = (ids[:, 0:1] == iota((SRC, CHANNELS), 1).astype(f32)).astype(f32).astype(bf16)
    used = iota((SRC, WIDE), 1) % LANES < USED
    src_ref[...] = jnp.where(used, dot(pick, given_ref[...]), 0.0).astype(bf16)
    src_lane = iota((256, SRC), 1).astype(f32)
    recv_lane = (iota((256, 256), 1) - iota((256, 256), 0) // CH_DEV * CH_DEV).astype(f32)
    bin_row = (iota((BINS, 256), 0) - BINS // 2).astype(f32).astype(bf16)
    one, zero = jnp.ones((BINS, 256), bf16), jnp.zeros((BINS, 256), bf16)
    for half in range(2):
        block = slice(256 * half, 256 * (half + 1))
        columns = given_ref[block, :LANES].astype(f32)
        spots = given_ref[block, LANES:].astype(f32).T
        for group in range(4):
            products, matches = [], []
            for j in range(4 * group, 4 * group + 4):
                pick_r = (columns[:, USED + j : USED + j + 1] == recv_lane).astype(f32).astype(bf16)
                pick_s = (columns[:, USED + 16 + j : USED + 17 + j] == src_lane).astype(f32).astype(bf16)
                r, s = dot(pick_r, given_ref[block, :]), dot(pick_s, src_ref[...])
                rc, rs, sc, ss = r[:, :LANES], r[:, LANES:], s[:, :LANES], s[:, LANES:]
                product = jnp.concatenate([rc * sc + rs * ss, rs * sc - rc * ss], axis=1)
                products.append(product.astype(bf16))
                matches.append(jnp.where(bin_row == spots[USED + j : USED + j + 1, :].astype(bf16), one, zero))
            part = dot(jnp.concatenate(matches, axis=1), jnp.concatenate(products, axis=0))
            if half == 0 and group == 0:
                total_ref[...] = part
            elif half == 1 and group == 3:
                pack(total_ref[...] + part, out_ref)
            else:
                total_ref[...] += part


def bin_pairs(given, ids):
    return pl.pallas_call(
        pairs_kernel,
        out_shape=jax.ShapeDtypeStruct((8, 48, WIDE), bf16),
        in_specs=[VMEM, VMEM],
        out_specs=VMEM,
        scratch_shapes=[pltpu.VMEM((SRC, WIDE), bf16), pltpu.VMEM((BINS, WIDE), f32)],
        compiler_params=pltpu.CompilerParams(vmem_limit_bytes=32 << 20),
        name="bin_pairs",
    )(given, ids)


def inverse_kernel(parts_ref, base_ref, turns_ref, out_ref):
    spectrum = unpack(jnp.sum(parts_ref[...].astype(f32), axis=0))
    high = spectrum.astype(bf16)
    low = (spectrum - high.astype(f32)).astype(bf16)
    both = jnp.concatenate([high, low], axis=0)
    count = high.shape[0]
    turn = iota((1, LAGS), 1) % 4
    sign = (1 - 2 * (turn % 2)).astype(f32)
    even = jnp.where(turn == 0, 1.0, jnp.where(turn == 2, -1.0, 0.0))
    odd = jnp.where(turn == 1, 1.0, jnp.where(turn == 3, -1.0, 0.0))
    gap = jnp.zeros((LANES - USED, LAGS), f32)
    real, imag = 0.0, 0.0
    for i, left in enumerate((both, high)):
        cos, sin = base_ref[i, :SLOTS, :].astype(f32), base_ref[i, SLOTS:, :].astype(f32)
        coses = [cos, sign * cos, even * cos - odd * sin, even * cos + odd * sin, gap]
        sines = [sin, sign * sin, even * sin + odd * cos, even * sin - odd * cos, gap]
        for_real = jnp.concatenate(coses + [-item for item in sines], axis=0).astype(bf16)
        for_imag = jnp.concatenate(sines + coses, axis=0).astype(bf16)
        a, b = dot(left, for_real), dot(left, for_imag)
        real, imag = real + a[:count], imag + b[:count]
        if i == 0:
            real, imag = real + a[count:], imag + b[count:]
    turns = turns_ref[lax.axis_index("zl")]
    lags = real * turns[0:1] - imag * turns[1:2]
    for zh in range(2):
        for group in range(8):
            tile = lags[32 * zh : 32 * (zh + 1), LANES * group : LANES * (group + 1)]
            for quarter in range(4):
                lane = slice(32 * quarter, 32 * (quarter + 1))
                pieces = [tile[8 * c : 8 * c + 8, lane] for c in range(4)]
                out_ref[32 * zh + 4 * ((4 * group + quarter) % 8) + group // 2] = jnp.concatenate(pieces, axis=1).astype(bf16)


def invert(parts):
    base, turns = inverse_tables()
    return pl.pallas_call(
        inverse_kernel,
        out_shape=jax.ShapeDtypeStruct((64, 8, LANES), bf16),
        in_specs=[VMEM, VMEM, VMEM],
        out_specs=VMEM,
        compiler_params=pltpu.CompilerParams(vmem_limit_bytes=32 << 20),
        name="invert",
    )(parts, jnp.asarray(base), jnp.asarray(turns))


def exchange(value, axes):
    return lax.all_to_all(value, axes, split_axis=0, concat_axis=0, tiled=True)


def shards(records, source_ids, pair_rows, pair_bins, bin_places):
    spectra = make_spectra(records.reshape(CH_DEV, NT), pair_rows, pair_bins, bin_places.reshape(1, BINS))
    given = exchange(spectra, ("zl", "x")).reshape(CHANNELS, WIDE)
    parts = exchange(bin_pairs(given, source_ids), ("y", "core"))
    shares = exchange(invert(parts), ("zh", "zl", "x"))
    return jnp.sum(shares.astype(f32), axis=0).reshape(BIN_DEV, 32)


def solution(mesh):
    fine = Mesh(mesh.devices.reshape(4, 8, 4, 2, 2), ("x", "zl", "y", "zh", "core"))
    chan, tm = ("x", "zl"), ("y", "zh", "core")
    in_specs = (P(chan, tm, None), P(), P(None, chan), P(None, chan), P())
    return jax.shard_map(shards, mesh=fine, in_specs=in_specs, out_specs=P(tm, chan), check_vma=False)
```

```python
import functools

import jax
import jax.numpy as jnp
import numpy as np
from jax import lax
from jax.experimental import pallas as pl
from jax.experimental.pallas import tpu as pltpu
from jax.sharding import Mesh, PartitionSpec as P

NT = 768
LAGS = 1024
SRC = 128
CH_DEV = 16
CHANNELS = 512
BIN_DEV = 32
BINS = 512
PAIRS = 1024
NFFT = 1536
PARTS = 8
SLOTS = NFFT // 8 // PARTS
USED = 4 * SLOTS
CUTS = 4
LANES = 128
WIDE = 2 * LANES

bf16 = jnp.bfloat16
f32 = jnp.float32
dot = functools.partial(jnp.dot, preferred_element_type=f32)
HBM = pl.BlockSpec(memory_space=pltpu.MemorySpace.HBM)
VMEM = pl.BlockSpec(memory_space=pltpu.VMEM)


def iota(shape, axis):
    return lax.broadcasted_iota(jnp.int32, shape, axis)


def angles(left, right):
    return (np.outer(left, right) % (2 * NFFT)) * (np.pi / NFFT)


def two_parts(exact):
    high = exact.astype(bf16)
    return np.stack([high, (exact - high.astype(np.float64)).astype(bf16)])


def forward_table():
    phase = angles(np.arange(NT), 2 * np.arange(NFFT // 8) + 1)
    return two_parts(np.concatenate([np.cos(phase), np.sin(phase)], axis=1))


def inverse_tables():
    lag = np.arange(LAGS) - LAGS // 2
    phase = angles(2 * np.arange(SLOTS) + 1, lag)
    turn = angles(np.arange(PARTS) * 2 * SLOTS, lag)
    scale = 2.0 / (NFFT * NT)
    turns = scale * np.stack([np.cos(turn), np.sin(turn)], axis=1)
    return two_parts(np.concatenate([np.cos(phase), np.sin(phase)], axis=0)), turns.astype(np.float32)


def spectra_kernel(records_hbm, table_hbm, rows_hbm, bins_hbm, places_hbm, out_ref, *scratch):
    *refs, sems = scratch
    rows_ref, bins_ref, places_ref, records_ref, table_ref = refs
    ends = [(rows_hbm, rows_ref), (bins_hbm, bins_ref), (places_hbm, places_ref), (records_hbm, records_ref)]
    for i in range(CUTS):
        cut = pl.ds(i * NT // CUTS, NT // CUTS)
        ends.append((table_hbm.at[:, cut, :], table_ref.at[:, cut, :]))
    copies = [pltpu.make_async_copy(source, target, sems.at[i]) for i, (source, target) in enumerate(ends)]
    for copy in copies:
        copy.start()
    for copy in copies[:3]:
        copy.wait()

    place = places_ref[...]
    owner, slot = place // BIN_DEV, place % BIN_DEV
    order = (owner % 2) * 256 + (owner // 4) * 64 + ((owner // 2) % 2) * 32 + (slot % 4) * 8 + slot // 4
    digits = jnp.broadcast_to(order - BINS // 2, (8, BINS)).astype(f32).astype(bf16)
    bins = (jnp.concatenate([bins_ref[0:1, :], bins_ref[1:2, :]], axis=1) - BINS // 2).astype(f32).astype(bf16)
    each = (iota((BINS, PAIRS), 0) - BINS // 2).astype(f32).astype(bf16)
    match = jnp.where(each == bins, jnp.ones((BINS, PAIRS), bf16), jnp.zeros((BINS, PAIRS), bf16))
    spots = dot(digits, match)[0:1]
    rows = jnp.concatenate([rows_ref[0:1, :], rows_ref[1:2, :]], axis=1)

    chosen = iota((PAIRS // 16, PAIRS), 0) == iota((PAIRS // 16, PAIRS), 1) // 16

    def spread(values, first_lane):
        kept = jnp.where(chosen, values, 0.0).astype(bf16)
        lane = (iota((PAIRS, LANES), 0) % 16 + first_lane == iota((PAIRS, LANES), 1)).astype(f32).astype(bf16)
        return dot(kept, lane)

    lists_1 = spread((rows // SRC).astype(f32), USED) + spread((rows % SRC).astype(f32), USED + 16)
    lists_2 = spread(spots, USED)

    copies[3].wait()
    values = records_ref[...].astype(f32)
    mean_square = jnp.mean(values * values, axis=-1, keepdims=True)
    normed = values * lax.rsqrt(mean_square + 1e-06)
    turn = iota(normed.shape, 1) % 4
    split = jnp.concatenate([jnp.where(turn == k, normed, 0.0) for k in range(4)], axis=0).astype(bf16)
    for copy in copies[4:]:
        copy.wait()
    sums = dot(split, table_ref[0]) + dot(split, table_ref[1])
    half = PARTS * SLOTS
    c0, c1, c2, c3 = (sums[CH_DEV * k : CH_DEV * (k + 1), :half] for k in range(4))
    s0, s1, s2, s3 = (sums[CH_DEV * k : CH_DEV * (k + 1), half:] for k in range(4))
    cosines = (c0 + c2 + c1 + c3, c0 + c2 - c1 - c3, c0 - c2 - s1 + s3, c0 - c2 + s1 - s3)
    sines = (s0 + s2 + s1 + s3, s0 + s2 - s1 - s3, s0 - s2 + c1 - c3, s0 - s2 - c1 + c3)
    gap = jnp.zeros((CH_DEV, LANES - USED), f32)
    for z in range(PARTS):
        cut = slice(SLOTS * z, SLOTS * (z + 1))
        parts = [jnp.concatenate([item[:, cut] for item in items] + [gap], axis=1) for items in (cosines, sines)]
        for x in range(4):
            rows_x = slice(CH_DEV * x, CH_DEV * (x + 1))
            full = jnp.concatenate([parts[0] + lists_1[rows_x], parts[1] + lists_2[rows_x]], axis=1)
            out_ref[4 * z + x] = full.astype(bf16)


def make_spectra(records, rows, bins, places):
    table = jnp.asarray(forward_table())
    inputs = (rows, bins, places, records, table)
    rows, bins, places, records, table = (pltpu.with_memory_space_constraint(item, pltpu.HBM) for item in inputs)
    return pl.pallas_call(
        spectra_kernel,
        out_shape=jax.ShapeDtypeStruct((4 * PARTS, CH_DEV, WIDE), bf16),
        in_specs=[HBM] * 5,
        out_specs=VMEM,
        scratch_shapes=[pltpu.VMEM(item.shape, item.dtype) for item in inputs] + [
            pltpu.SemaphoreType.DMA((4 + CUTS,))
        ],
        compiler_params=pltpu.CompilerParams(vmem_limit_bytes=16 << 20),
        name="spectra",
    )(records, table, rows, bins, places)


def pack(total, out_ref):
    for i in range(8):
        kept, moved = total[64 * i : 64 * i + 48], total[64 * i + 48 : 64 * i + 64]
        tiles = []
        for start in (0, LANES):
            thirds = [moved[:, start + 32 * k : start + 32 * (k + 1)] for k in range(3)]
            tiles += [kept[:, start : start + USED], jnp.concatenate(thirds, axis=0)]
        out_ref[i] = jnp.concatenate(tiles, axis=1).astype(bf16)


def unpack(packed):
    moved = []
    for start in (0, LANES):
        spare = packed[:, start + USED : start + LANES]
        thirds = [spare[16 * k : 16 * (k + 1)] for k in range(3)]
        moved += thirds + [jnp.zeros((16, LANES - USED), f32)]
    return jnp.concatenate([packed, jnp.concatenate(moved, axis=1)], axis=0)


def pairs_kernel(given_ref, ids_ref, out_ref, src_ref, total_ref):
    ids = ids_ref[pl.ds(lax.axis_index("x") // 2, 1), :]
    block = ids // CH_DEV
    ids = (block % PARTS * 4 + block // PARTS) * CH_DEV + ids % CH_DEV
    ids = jnp.broadcast_to(ids.astype(f32), (8, SRC)).T
    pick = (ids[:, 0:1] == iota((SRC, CHANNELS), 1).astype(f32)).astype(f32).astype(bf16)
    used = iota((SRC, WIDE), 1) % LANES < USED
    src_ref[...] = jnp.where(used, dot(pick, given_ref[...]), 0.0).astype(bf16)
    src_lane = iota((256, SRC), 1).astype(f32)
    recv_lane = (iota((256, 256), 1) - iota((256, 256), 0) // CH_DEV * CH_DEV).astype(f32)
    bin_row = (iota((BINS, 256), 0) - BINS // 2).astype(f32).astype(bf16)
    one, zero = jnp.ones((BINS, 256), bf16), jnp.zeros((BINS, 256), bf16)
    for half in range(2):
        block = slice(256 * half, 256 * (half + 1))
        columns = given_ref[block, :LANES].astype(f32)
        spots = given_ref[block, LANES:].astype(f32).T
        for group in range(4):
            products, matches = [], []
            for j in range(4 * group, 4 * group + 4):
                pick_r = (columns[:, USED + j : USED + j + 1] == recv_lane).astype(f32).astype(bf16)
                pick_s = (columns[:, USED + 16 + j : USED + 17 + j] == src_lane).astype(f32).astype(bf16)
                r, s = dot(pick_r, given_ref[block, :]), dot(pick_s, src_ref[...])
                rc, rs, sc, ss = r[:, :LANES], r[:, LANES:], s[:, :LANES], s[:, LANES:]
                product = jnp.concatenate([rc * sc + rs * ss, rs * sc - rc * ss], axis=1)
                products.append(product.astype(bf16))
                matches.append(jnp.where(bin_row == spots[USED + j : USED + j + 1, :].astype(bf16), one, zero))
            part = dot(jnp.concatenate(matches, axis=1), jnp.concatenate(products, axis=0))
            if half == 0 and group == 0:
                total_ref[...] = part
            elif half == 1 and group == 3:
                pack(total_ref[...] + part, out_ref)
            else:
                total_ref[...] += part


def bin_pairs(given, ids):
    return pl.pallas_call(
        pairs_kernel,
        out_shape=jax.ShapeDtypeStruct((8, 48, WIDE), bf16),
        in_specs=[VMEM, VMEM],
        out_specs=VMEM,
        scratch_shapes=[pltpu.VMEM((SRC, WIDE), bf16), pltpu.VMEM((BINS, WIDE), f32)],
        compiler_params=pltpu.CompilerParams(vmem_limit_bytes=32 << 20),
        name="bin_pairs",
    )(given, ids)


def inverse_kernel(parts_ref, base_ref, turns_ref, out_ref):
    spectrum = unpack(jnp.sum(parts_ref[...].astype(f32), axis=0))
    high = spectrum.astype(bf16)
    low = (spectrum - high.astype(f32)).astype(bf16)
    both = jnp.concatenate([high, low], axis=0)
    count = high.shape[0]
    turn = iota((1, LAGS), 1) % 4
    sign = (1 - 2 * (turn % 2)).astype(f32)
    even = jnp.where(turn == 0, 1.0, jnp.where(turn == 2, -1.0, 0.0))
    odd = jnp.where(turn == 1, 1.0, jnp.where(turn == 3, -1.0, 0.0))
    gap = jnp.zeros((LANES - USED, LAGS), f32)
    real, imag = 0.0, 0.0
    for i, left in enumerate((both, high)):
        cos, sin = base_ref[i, :SLOTS, :].astype(f32), base_ref[i, SLOTS:, :].astype(f32)
        coses = [cos, sign * cos, even * cos - odd * sin, even * cos + odd * sin, gap]
        sines = [sin, sign * sin, even * sin + odd * cos, even * sin - odd * cos, gap]
        for_real = jnp.concatenate(coses + [-item for item in sines], axis=0).astype(bf16)
        for_imag = jnp.concatenate(sines + coses, axis=0).astype(bf16)
        a, b = dot(left, for_real), dot(left, for_imag)
        real, imag = real + a[:count], imag + b[:count]
        if i == 0:
            real, imag = real + a[count:], imag + b[count:]
    turns = turns_ref[lax.axis_index("zl")]
    lags = real * turns[0:1] - imag * turns[1:2]
    for zh in range(2):
        for group in range(8):
            tile = lags[32 * zh : 32 * (zh + 1), LANES * group : LANES * (group + 1)]
            for quarter in range(4):
                lane = slice(32 * quarter, 32 * (quarter + 1))
                pieces = [tile[8 * c : 8 * c + 8, lane] for c in range(4)]
                out_ref[32 * zh + 4 * ((4 * group + quarter) % 8) + group // 2] = jnp.concatenate(pieces, axis=1).astype(bf16)


def invert(parts):
    base, turns = inverse_tables()
    return pl.pallas_call(
        inverse_kernel,
        out_shape=jax.ShapeDtypeStruct((64, 8, LANES), bf16),
        in_specs=[VMEM, VMEM, VMEM],
        out_specs=VMEM,
        compiler_params=pltpu.CompilerParams(vmem_limit_bytes=32 << 20),
        name="invert",
    )(parts, jnp.asarray(base), jnp.asarray(turns))


def exchange(value, axes):
    return lax.all_to_all(value, axes, split_axis=0, concat_axis=0, tiled=True)


def shards(records, source_ids, pair_rows, pair_bins, bin_places):
    spectra = make_spectra(records.reshape(CH_DEV, NT), pair_rows, pair_bins, bin_places.reshape(1, BINS))
    given = exchange(spectra, ("zl", "x")).reshape(CHANNELS, WIDE)
    parts = exchange(bin_pairs(given, source_ids), ("core", "y"))
    shares = exchange(invert(parts), ("zh", "zl", "x"))
    return jnp.sum(shares.astype(f32), axis=0).reshape(BIN_DEV, 32)


def solution(mesh):
    fine = Mesh(mesh.devices.reshape(4, 8, 4, 2, 2), ("x", "zl", "y", "zh", "core"))
    chan, tm = ("x", "zl"), ("y", "zh", "core")
    in_specs = (P(chan, tm, None), P(), P(None, chan), P(None, chan), P())
    return jax.shard_map(shards, mesh=fine, in_specs=in_specs, out_specs=P(tm, chan), check_vma=False)
```

```python
import functools

import jax
import jax.numpy as jnp
import numpy as np
from jax import lax
from jax.experimental import pallas as pl
from jax.experimental.pallas import tpu as pltpu
from jax.sharding import Mesh, PartitionSpec as P

NT = 768
LAGS = 1024
SRC = 128
CH_DEV = 16
CHANNELS = 512
BIN_DEV = 32
BINS = 512
PAIRS = 1024
NFFT = 1536
PARTS = 8
SLOTS = NFFT // 8 // PARTS
USED = 4 * SLOTS
CUTS = 4
LANES = 128
WIDE = 2 * LANES

bf16 = jnp.bfloat16
f32 = jnp.float32
dot = functools.partial(jnp.dot, preferred_element_type=f32)
HBM = pl.BlockSpec(memory_space=pltpu.MemorySpace.HBM)
VMEM = pl.BlockSpec(memory_space=pltpu.VMEM)


def iota(shape, axis):
    return lax.broadcasted_iota(jnp.int32, shape, axis)


def angles(left, right):
    return (np.outer(left, right) % (2 * NFFT)) * (np.pi / NFFT)


def two_parts(exact):
    high = exact.astype(bf16)
    return np.stack([high, (exact - high.astype(np.float64)).astype(bf16)])


def forward_table():
    phase = angles(np.arange(NT), 2 * np.arange(NFFT // 8) + 1)
    return two_parts(np.concatenate([np.cos(phase), np.sin(phase)], axis=1))


def inverse_tables():
    lag = np.arange(LAGS) - LAGS // 2
    phase = angles(2 * np.arange(SLOTS) + 1, lag)
    turn = angles(np.arange(PARTS) * 2 * SLOTS, lag)
    scale = 2.0 / (NFFT * NT)
    turns = scale * np.stack([np.cos(turn), np.sin(turn)], axis=1)
    return two_parts(np.concatenate([np.cos(phase), np.sin(phase)], axis=0)), turns.astype(np.float32)


def spectra_kernel(records_hbm, table_hbm, rows_hbm, bins_hbm, places_hbm, out_ref, *scratch):
    *refs, sems = scratch
    rows_ref, bins_ref, places_ref, records_ref, table_ref = refs
    ends = [(rows_hbm, rows_ref), (bins_hbm, bins_ref), (places_hbm, places_ref), (records_hbm, records_ref)]
    for i in range(CUTS):
        cut = pl.ds(i * NT // CUTS, NT // CUTS)
        ends.append((table_hbm.at[:, cut, :], table_ref.at[:, cut, :]))
    copies = [pltpu.make_async_copy(source, target, sems.at[i]) for i, (source, target) in enumerate(ends)]
    for copy in copies:
        copy.start()
    for copy in copies[:3]:
        copy.wait()

    place = places_ref[...]
    owner, slot = place // BIN_DEV, place % BIN_DEV
    order = (owner // 4) * 128 + (owner % 2) * 64 + ((owner // 2) % 2) * 32 + slot
    digits = jnp.broadcast_to(order - BINS // 2, (8, BINS)).astype(f32).astype(bf16)
    bins = jnp.concatenate([bins_ref[0:1, :], bins_ref[1:2, :]], axis=1)
    spots = dot(digits, (iota((BINS, PAIRS), 0) == bins).astype(f32).astype(bf16))[0:1]
    rows = jnp.concatenate([rows_ref[0:1, :], rows_ref[1:2, :]], axis=1)

    chosen = iota((PAIRS // 16, PAIRS), 0) == iota((PAIRS // 16, PAIRS), 1) // 16

    def spread(values, first_lane):
        kept = jnp.where(chosen, values, 0.0).astype(bf16)
        lane = (iota((PAIRS, LANES), 0) % 16 + first_lane == iota((PAIRS, LANES), 1)).astype(f32).astype(bf16)
        return dot(kept, lane)

    lists_1 = spread((rows // SRC).astype(f32), USED) + spread((rows % SRC).astype(f32), USED + 16)
    lists_2 = spread(spots, USED)

    copies[3].wait()
    values = records_ref[...].astype(f32)
    mean_square = jnp.mean(values * values, axis=-1, keepdims=True)
    normed = values * lax.rsqrt(mean_square + 1e-06)
    turn = iota(normed.shape, 1) % 4
    split = jnp.concatenate([jnp.where(turn == k, normed, 0.0) for k in range(4)], axis=0).astype(bf16)
    for copy in copies[4:]:
        copy.wait()
    sums = dot(split, table_ref[0]) + dot(split, table_ref[1])
    half = PARTS * SLOTS
    c0, c1, c2, c3 = (sums[CH_DEV * k : CH_DEV * (k + 1), :half] for k in range(4))
    s0, s1, s2, s3 = (sums[CH_DEV * k : CH_DEV * (k + 1), half:] for k in range(4))
    cosines = (c0 + c2 + c1 + c3, c0 + c2 - c1 - c3, c0 - c2 - s1 + s3, c0 - c2 + s1 - s3)
    sines = (s0 + s2 + s1 + s3, s0 + s2 - s1 - s3, s0 - s2 + c1 - c3, s0 - s2 - c1 + c3)
    gap = jnp.zeros((CH_DEV, LANES - USED), f32)
    for z in range(PARTS):
        cut = slice(SLOTS * z, SLOTS * (z + 1))
        parts = [jnp.concatenate([item[:, cut] for item in items] + [gap], axis=1) for items in (cosines, sines)]
        for x in range(4):
            rows_x = slice(CH_DEV * x, CH_DEV * (x + 1))
            full = jnp.concatenate([parts[0] + lists_1[rows_x], parts[1] + lists_2[rows_x]], axis=1)
            out_ref[4 * z + x] = full.astype(bf16)


def make_spectra(records, rows, bins, places):
    table = jnp.asarray(forward_table())
    inputs = (rows, bins, places, records, table)
    rows, bins, places, records, table = (pltpu.with_memory_space_constraint(item, pltpu.HBM) for item in inputs)
    return pl.pallas_call(
        spectra_kernel,
        out_shape=jax.ShapeDtypeStruct((4 * PARTS, CH_DEV, WIDE), bf16),
        in_specs=[HBM] * 5,
        out_specs=VMEM,
        scratch_shapes=[pltpu.VMEM(item.shape, item.dtype) for item in inputs] + [
            pltpu.SemaphoreType.DMA((4 + CUTS,))
        ],
        compiler_params=pltpu.CompilerParams(vmem_limit_bytes=16 << 20),
        name="spectra",
    )(records, table, rows, bins, places)


def pack(total, out_ref):
    for i in range(8):
        kept, moved = total[64 * i : 64 * i + 48], total[64 * i + 48 : 64 * i + 64]
        tiles = []
        for start in (0, LANES):
            thirds = [moved[:, start + 32 * k : start + 32 * (k + 1)] for k in range(3)]
            tiles += [kept[:, start : start + USED], jnp.concatenate(thirds, axis=0)]
        out_ref[i] = jnp.concatenate(tiles, axis=1).astype(bf16)


def unpack(packed):
    moved = []
    for start in (0, LANES):
        spare = packed[:, start + USED : start + LANES]
        thirds = [spare[16 * k : 16 * (k + 1)] for k in range(3)]
        moved += thirds + [jnp.zeros((16, LANES - USED), f32)]
    return jnp.concatenate([packed, jnp.concatenate(moved, axis=1)], axis=0)


def pairs_kernel(given_ref, ids_ref, out_ref, src_ref, total_ref):
    ids = ids_ref[pl.ds(lax.axis_index("x") // 2, 1), :]
    block = ids // CH_DEV
    ids = (block % PARTS * 4 + block // PARTS) * CH_DEV + ids % CH_DEV
    ids = jnp.broadcast_to(ids.astype(f32), (8, SRC)).T
    pick = (ids[:, 0:1] == iota((SRC, CHANNELS), 1).astype(f32)).astype(f32).astype(bf16)
    used = iota((SRC, WIDE), 1) % LANES < USED
    src_ref[...] = jnp.where(used, dot(pick, given_ref[...]), 0.0).astype(bf16)
    src_lane = iota((256, SRC), 1).astype(f32)
    recv_lane = (iota((256, 256), 1) - iota((256, 256), 0) // CH_DEV * CH_DEV).astype(f32)
    bin_row = (iota((BINS, 256), 0) - BINS // 2).astype(f32).astype(bf16)
    one, zero = jnp.ones((BINS, 256), bf16), jnp.zeros((BINS, 256), bf16)
    for half in range(2):
        block = slice(256 * half, 256 * (half + 1))
        columns = given_ref[block, :LANES].astype(f32)
        spots = given_ref[block, LANES:].astype(f32).T
        for group in range(4):
            products, matches = [], []
            for j in range(4 * group, 4 * group + 4):
                pick_r = (columns[:, USED + j : USED + j + 1] == recv_lane).astype(f32).astype(bf16)
                pick_s = (columns[:, USED + 16 + j : USED + 17 + j] == src_lane).astype(f32).astype(bf16)
                r, s = dot(pick_r, given_ref[block, :]), dot(pick_s, src_ref[...])
                rc, rs, sc, ss = r[:, :LANES], r[:, LANES:], s[:, :LANES], s[:, LANES:]
                product = jnp.concatenate([rc * sc + rs * ss, rs * sc - rc * ss], axis=1)
                products.append(product.astype(bf16))
                matches.append(jnp.where(bin_row == spots[USED + j : USED + j + 1, :].astype(bf16), one, zero))
            part = dot(jnp.concatenate(matches, axis=1), jnp.concatenate(products, axis=0))
            if half == 0 and group == 0:
                total_ref[...] = part
            elif half == 1 and group == 3:
                pack(total_ref[...] + part, out_ref)
            else:
                total_ref[...] += part


def bin_pairs(given, ids):
    return pl.pallas_call(
        pairs_kernel,
        out_shape=jax.ShapeDtypeStruct((8, 48, WIDE), bf16),
        in_specs=[VMEM, VMEM],
        out_specs=VMEM,
        scratch_shapes=[pltpu.VMEM((SRC, WIDE), bf16), pltpu.VMEM((BINS, WIDE), f32)],
        compiler_params=pltpu.CompilerParams(vmem_limit_bytes=32 << 20),
        name="bin_pairs",
    )(given, ids)


def inverse_kernel(parts_ref, base_ref, turns_ref, out_ref):
    spectrum = unpack(jnp.sum(parts_ref[...].astype(f32), axis=0))
    high = spectrum.astype(bf16)
    low = (spectrum - high.astype(f32)).astype(bf16)
    both = jnp.concatenate([high, low], axis=0)
    count = high.shape[0]
    turn = iota((1, LAGS), 1) % 4
    sign = (1 - 2 * (turn % 2)).astype(f32)
    even = jnp.where(turn == 0, 1.0, jnp.where(turn == 2, -1.0, 0.0))
    odd = jnp.where(turn == 1, 1.0, jnp.where(turn == 3, -1.0, 0.0))
    gap = jnp.zeros((LANES - USED, LAGS), f32)
    real, imag = 0.0, 0.0
    for i, left in enumerate((both, high)):
        cos, sin = base_ref[i, :SLOTS, :].astype(f32), base_ref[i, SLOTS:, :].astype(f32)
        coses = [cos, sign * cos, even * cos - odd * sin, even * cos + odd * sin, gap]
        sines = [sin, sign * sin, even * sin + odd * cos, even * sin - odd * cos, gap]
        for_real = jnp.concatenate(coses + [-item for item in sines], axis=0).astype(bf16)
        for_imag = jnp.concatenate(sines + coses, axis=0).astype(bf16)
        a, b = dot(left, for_real), dot(left, for_imag)
        real, imag = real + a[:count], imag + b[:count]
        if i == 0:
            real, imag = real + a[count:], imag + b[count:]
    turns = turns_ref[lax.axis_index("zl")]
    lags = real * turns[0:1] - imag * turns[1:2]
    for zh in range(2):
        for group in range(8):
            tile = lags[32 * zh : 32 * (zh + 1), LANES * group : LANES * (group + 1)]
            for quarter in range(4):
                lane = slice(32 * quarter, 32 * (quarter + 1))
                pieces = [tile[8 * c : 8 * c + 8, lane] for c in range(4)]
                out_ref[32 * zh + 4 * ((4 * group + quarter) % 8) + group // 2] = jnp.concatenate(pieces, axis=1).astype(bf16)


def invert(parts):
    base, turns = inverse_tables()
    return pl.pallas_call(
        inverse_kernel,
        out_shape=jax.ShapeDtypeStruct((64, 8, LANES), bf16),
        in_specs=[VMEM, VMEM, VMEM],
        out_specs=VMEM,
        compiler_params=pltpu.CompilerParams(vmem_limit_bytes=32 << 20),
        name="invert",
    )(parts, jnp.asarray(base), jnp.asarray(turns))


def sum_kernel(shares_ref, out_ref):
    total = jnp.sum(shares_ref[...].astype(f32), axis=0)
    for c in range(4):
        out_ref[8 * c : 8 * c + 8, :] = total[:, 32 * c : 32 * c + 32]


def sum_shares(shares):
    return pl.pallas_call(
        sum_kernel,
        out_shape=jax.ShapeDtypeStruct((BIN_DEV, 32), f32),
        in_specs=[VMEM],
        out_specs=VMEM,
        compiler_params=pltpu.CompilerParams(vmem_limit_bytes=16 << 20),
        name="sum_shares",
    )(shares)


def exchange(value, axes):
    return lax.all_to_all(value, axes, split_axis=0, concat_axis=0, tiled=True)


def shards(records, source_ids, pair_rows, pair_bins, bin_places):
    spectra = make_spectra(records.reshape(CH_DEV, NT), pair_rows, pair_bins, bin_places.reshape(1, BINS))
    given = exchange(spectra, ("zl", "x")).reshape(CHANNELS, WIDE)
    parts = exchange(bin_pairs(given, source_ids), ("y", "core"))
    return sum_shares(exchange(invert(parts), ("zh", "zl", "x")))


def solution(mesh):
    fine = Mesh(mesh.devices.reshape(4, 8, 4, 2, 2), ("x", "zl", "y", "zh", "core"))
    chan, tm = ("x", "zl"), ("y", "zh", "core")
    in_specs = (P(chan, tm, None), P(), P(None, chan), P(None, chan), P())
    return jax.shard_map(shards, mesh=fine, in_specs=in_specs, out_specs=P(tm, chan), check_vma=False)
```

```python
import functools

import jax
import jax.numpy as jnp
import numpy as np
from jax import lax
from jax.experimental import pallas as pl
from jax.experimental.pallas import tpu as pltpu
from jax.sharding import Mesh, PartitionSpec as P

NT = 768
LAGS = 1024
SRC = 128
CH_DEV = 16
CHANNELS = 512
BIN_DEV = 32
BINS = 512
PAIRS = 1024
NFFT = 1536
PARTS = 8
SLOTS = NFFT // 8 // PARTS
USED = 4 * SLOTS
CUTS = 2
LANES = 128
WIDE = 2 * LANES

bf16 = jnp.bfloat16
f32 = jnp.float32
dot = functools.partial(jnp.dot, preferred_element_type=f32)
HBM = pl.BlockSpec(memory_space=pltpu.MemorySpace.HBM)
VMEM = pl.BlockSpec(memory_space=pltpu.VMEM)


def iota(shape, axis):
    return lax.broadcasted_iota(jnp.int32, shape, axis)


def angles(left, right):
    return (np.outer(left, right) % (2 * NFFT)) * (np.pi / NFFT)


def two_parts(exact):
    high = exact.astype(bf16)
    return np.stack([high, (exact - high.astype(np.float64)).astype(bf16)])


def forward_table():
    phase = angles(np.arange(NT), 2 * np.arange(NFFT // 8) + 1)
    return two_parts(np.concatenate([np.cos(phase), np.sin(phase)], axis=1))


def inverse_tables():
    lag = np.arange(LAGS) - LAGS // 2
    phase = angles(2 * np.arange(SLOTS) + 1, lag)
    turn = angles(np.arange(PARTS) * 2 * SLOTS, lag)
    scale = 2.0 / (NFFT * NT)
    turns = scale * np.stack([np.cos(turn), np.sin(turn)], axis=1)
    return two_parts(np.concatenate([np.cos(phase), np.sin(phase)], axis=0)), turns.astype(np.float32)


def spectra_kernel(records_hbm, table_hbm, rows_hbm, bins_hbm, places_hbm, out_ref, *scratch):
    *refs, sems = scratch
    rows_ref, bins_ref, places_ref, records_ref, table_ref = refs
    ends = [(rows_hbm, rows_ref), (bins_hbm, bins_ref), (places_hbm, places_ref), (records_hbm, records_ref)]
    for i in range(CUTS):
        cut = pl.ds(i * NT // CUTS, NT // CUTS)
        ends.append((table_hbm.at[:, cut, :], table_ref.at[:, cut, :]))
    copies = [pltpu.make_async_copy(source, target, sems.at[i]) for i, (source, target) in enumerate(ends)]
    for copy in copies:
        copy.start()
    for copy in copies[:3]:
        copy.wait()

    place = places_ref[...]
    owner, slot = place // BIN_DEV, place % BIN_DEV
    order = (owner // 4) * 128 + (owner % 2) * 64 + ((owner // 2) % 2) * 32 + (slot % 4) * 8 + slot // 4
    digits = jnp.broadcast_to(order - BINS // 2, (8, BINS)).astype(f32).astype(bf16)
    bins = jnp.concatenate([bins_ref[0:1, :], bins_ref[1:2, :]], axis=1)
    spots = dot(digits, (iota((BINS, PAIRS), 0) == bins).astype(f32).astype(bf16))[0:1]
    rows = jnp.concatenate([rows_ref[0:1, :], rows_ref[1:2, :]], axis=1)

    chosen = iota((PAIRS // 16, PAIRS), 0) == iota((PAIRS // 16, PAIRS), 1) // 16

    def spread(values, first_lane):
        kept = jnp.where(chosen, values, 0.0).astype(bf16)
        lane = (iota((PAIRS, LANES), 0) % 16 + first_lane == iota((PAIRS, LANES), 1)).astype(f32).astype(bf16)
        return dot(kept, lane)

    lists_1 = spread((rows // SRC).astype(f32), USED) + spread((rows % SRC).astype(f32), USED + 16)
    lists_2 = spread(spots, USED)

    copies[3].wait()
    values = records_ref[...].astype(f32)
    mean_square = jnp.mean(values * values, axis=-1, keepdims=True)
    normed = values * lax.rsqrt(mean_square + 1e-06)
    turn = iota(normed.shape, 1) % 4
    split = jnp.concatenate([jnp.where(turn == k, normed, 0.0) for k in range(4)], axis=0).astype(bf16)
    for copy in copies[4:]:
        copy.wait()
    sums = dot(split, table_ref[0]) + dot(split, table_ref[1])
    half = PARTS * SLOTS
    c0, c1, c2, c3 = (sums[CH_DEV * k : CH_DEV * (k + 1), :half] for k in range(4))
    s0, s1, s2, s3 = (sums[CH_DEV * k : CH_DEV * (k + 1), half:] for k in range(4))
    cosines = (c0 + c2 + c1 + c3, c0 + c2 - c1 - c3, c0 - c2 - s1 + s3, c0 - c2 + s1 - s3)
    sines = (s0 + s2 + s1 + s3, s0 + s2 - s1 - s3, s0 - s2 + c1 - c3, s0 - s2 - c1 + c3)
    gap = jnp.zeros((CH_DEV, LANES - USED), f32)
    for z in range(PARTS):
        cut = slice(SLOTS * z, SLOTS * (z + 1))
        parts = [jnp.concatenate([item[:, cut] for item in items] + [gap], axis=1) for items in (cosines, sines)]
        for x in range(4):
            rows_x = slice(CH_DEV * x, CH_DEV * (x + 1))
            full = jnp.concatenate([parts[0] + lists_1[rows_x], parts[1] + lists_2[rows_x]], axis=1)
            out_ref[4 * z + x] = full.astype(bf16)


def make_spectra(records, rows, bins, places):
    table = jnp.asarray(forward_table())
    inputs = (rows, bins, places, records, table)
    rows, bins, places, records, table = (pltpu.with_memory_space_constraint(item, pltpu.HBM) for item in inputs)
    return pl.pallas_call(
        spectra_kernel,
        out_shape=jax.ShapeDtypeStruct((4 * PARTS, CH_DEV, WIDE), bf16),
        in_specs=[HBM] * 5,
        out_specs=VMEM,
        scratch_shapes=[pltpu.VMEM(item.shape, item.dtype) for item in inputs] + [
            pltpu.SemaphoreType.DMA((4 + CUTS,))
        ],
        compiler_params=pltpu.CompilerParams(vmem_limit_bytes=16 << 20),
        name="spectra",
    )(records, table, rows, bins, places)


def pack(total, out_ref):
    for i in range(8):
        kept, moved = total[64 * i : 64 * i + 48], total[64 * i + 48 : 64 * i + 64]
        tiles = []
        for start in (0, LANES):
            thirds = [moved[:, start + 32 * k : start + 32 * (k + 1)] for k in range(3)]
            tiles += [kept[:, start : start + USED], jnp.concatenate(thirds, axis=0)]
        out_ref[i] = jnp.concatenate(tiles, axis=1).astype(bf16)


def unpack(packed):
    moved = []
    for start in (0, LANES):
        spare = packed[:, start + USED : start + LANES]
        thirds = [spare[16 * k : 16 * (k + 1)] for k in range(3)]
        moved += thirds + [jnp.zeros((16, LANES - USED), f32)]
    return jnp.concatenate([packed, jnp.concatenate(moved, axis=1)], axis=0)


def pairs_kernel(given_ref, ids_ref, out_ref, src_ref, total_ref):
    ids = ids_ref[pl.ds(lax.axis_index("x") // 2, 1), :]
    block = ids // CH_DEV
    ids = (block % PARTS * 4 + block // PARTS) * CH_DEV + ids % CH_DEV
    ids = jnp.broadcast_to(ids.astype(f32), (8, SRC)).T
    pick = (ids[:, 0:1] == iota((SRC, CHANNELS), 1).astype(f32)).astype(f32).astype(bf16)
    used = iota((SRC, WIDE), 1) % LANES < USED
    src_ref[...] = jnp.where(used, dot(pick, given_ref[...]), 0.0).astype(bf16)
    src_lane = iota((256, SRC), 1).astype(f32)
    recv_lane = (iota((256, 256), 1) - iota((256, 256), 0) // CH_DEV * CH_DEV).astype(f32)
    bin_row = (iota((BINS, 256), 0) - BINS // 2).astype(f32).astype(bf16)
    one, zero = jnp.ones((BINS, 256), bf16), jnp.zeros((BINS, 256), bf16)
    for half in range(2):
        block = slice(256 * half, 256 * (half + 1))
        columns = given_ref[block, :LANES].astype(f32)
        spots = given_ref[block, LANES:].astype(f32).T
        for group in range(4):
            products, matches = [], []
            for j in range(4 * group, 4 * group + 4):
                pick_r = (columns[:, USED + j : USED + j + 1] == recv_lane).astype(f32).astype(bf16)
                pick_s = (columns[:, USED + 16 + j : USED + 17 + j] == src_lane).astype(f32).astype(bf16)
                r, s = dot(pick_r, given_ref[block, :]), dot(pick_s, src_ref[...])
                rc, rs, sc, ss = r[:, :LANES], r[:, LANES:], s[:, :LANES], s[:, LANES:]
                product = jnp.concatenate([rc * sc + rs * ss, rs * sc - rc * ss], axis=1)
                products.append(product.astype(bf16))
                matches.append(jnp.where(bin_row == spots[USED + j : USED + j + 1, :].astype(bf16), one, zero))
            part = dot(jnp.concatenate(matches, axis=1), jnp.concatenate(products, axis=0))
            if half == 0 and group == 0:
                total_ref[...] = part
            elif half == 1 and group == 3:
                pack(total_ref[...] + part, out_ref)
            else:
                total_ref[...] += part


def bin_pairs(given, ids):
    return pl.pallas_call(
        pairs_kernel,
        out_shape=jax.ShapeDtypeStruct((8, 48, WIDE), bf16),
        in_specs=[VMEM, VMEM],
        out_specs=VMEM,
        scratch_shapes=[pltpu.VMEM((SRC, WIDE), bf16), pltpu.VMEM((BINS, WIDE), f32)],
        compiler_params=pltpu.CompilerParams(vmem_limit_bytes=32 << 20),
        name="bin_pairs",
    )(given, ids)


def inverse_kernel(parts_ref, base_ref, turns_ref, out_ref):
    spectrum = unpack(jnp.sum(parts_ref[...].astype(f32), axis=0))
    high = spectrum.astype(bf16)
    low = (spectrum - high.astype(f32)).astype(bf16)
    both = jnp.concatenate([high, low], axis=0)
    count = high.shape[0]
    turn = iota((1, LAGS), 1) % 4
    sign = (1 - 2 * (turn % 2)).astype(f32)
    even = jnp.where(turn == 0, 1.0, jnp.where(turn == 2, -1.0, 0.0))
    odd = jnp.where(turn == 1, 1.0, jnp.where(turn == 3, -1.0, 0.0))
    gap = jnp.zeros((LANES - USED, LAGS), f32)
    real, imag = 0.0, 0.0
    for i, left in enumerate((both, high)):
        cos, sin = base_ref[i, :SLOTS, :].astype(f32), base_ref[i, SLOTS:, :].astype(f32)
        coses = [cos, sign * cos, even * cos - odd * sin, even * cos + odd * sin, gap]
        sines = [sin, sign * sin, even * sin + odd * cos, even * sin - odd * cos, gap]
        for_real = jnp.concatenate(coses + [-item for item in sines], axis=0).astype(bf16)
        for_imag = jnp.concatenate(sines + coses, axis=0).astype(bf16)
        a, b = dot(left, for_real), dot(left, for_imag)
        real, imag = real + a[:count], imag + b[:count]
        if i == 0:
            real, imag = real + a[count:], imag + b[count:]
    turns = turns_ref[lax.axis_index("zl")]
    lags = real * turns[0:1] - imag * turns[1:2]
    for zh in range(2):
        for group in range(8):
            tile = lags[32 * zh : 32 * (zh + 1), LANES * group : LANES * (group + 1)]
            for quarter in range(4):
                lane = slice(32 * quarter, 32 * (quarter + 1))
                pieces = [tile[8 * c : 8 * c + 8, lane] for c in range(4)]
                out_ref[32 * zh + 4 * ((4 * group + quarter) % 8) + group // 2] = jnp.concatenate(pieces, axis=1).astype(bf16)


def invert(parts):
    base, turns = inverse_tables()
    return pl.pallas_call(
        inverse_kernel,
        out_shape=jax.ShapeDtypeStruct((64, 8, LANES), bf16),
        in_specs=[VMEM, VMEM, VMEM],
        out_specs=VMEM,
        compiler_params=pltpu.CompilerParams(vmem_limit_bytes=32 << 20),
        name="invert",
    )(parts, jnp.asarray(base), jnp.asarray(turns))


def exchange(value, axes):
    return lax.all_to_all(value, axes, split_axis=0, concat_axis=0, tiled=True)


def shards(records, source_ids, pair_rows, pair_bins, bin_places):
    spectra = make_spectra(records.reshape(CH_DEV, NT), pair_rows, pair_bins, bin_places.reshape(1, BINS))
    given = exchange(spectra, ("zl", "x")).reshape(CHANNELS, WIDE)
    parts = exchange(bin_pairs(given, source_ids), ("y", "core"))
    shares = exchange(invert(parts), ("zh", "zl", "x"))
    return jnp.sum(shares.astype(f32), axis=0).reshape(BIN_DEV, 32)


def solution(mesh):
    fine = Mesh(mesh.devices.reshape(4, 8, 4, 2, 2), ("x", "zl", "y", "zh", "core"))
    chan, tm = ("x", "zl"), ("y", "zh", "core")
    in_specs = (P(chan, tm, None), P(), P(None, chan), P(None, chan), P())
    return jax.shard_map(shards, mesh=fine, in_specs=in_specs, out_specs=P(tm, chan), check_vma=False)
```
